512 devices in a mesh: gx: 4 (over x), gy: 4 (over y_lo, core), gz: 32 (over y_hi, z).
Axes of the slice: x: 4, y: 8 (y_hi: 4, y_lo: 2; y = y_hi * 2 + y_lo), z: 8, core: 2. Of those that a mesh axis runs over, the one named last changes fastest.
Arguments:
- field_h: float32 [10, 128, 32, 512], P(None, 'gz', 'gy', 'gx'), may hold values from -6 to 6
- field_p: float32 [10, 128, 32, 512], P(None, 'gz', 'gy', 'gx'), may hold values from -6 to 6
- potential: float32 [128, 32, 512], P('gz', 'gy', 'gx'), may hold values from 0.25 to 2.5
- coupling: float32 [10, 10], replicated, may hold values from -2 to 2
- wt_cells: int32 [32, 4, 4, 8, 128], P('gz', 'gy', 'gx'), may hold values from 0 to 4095
- wt_coords: float32 [32, 4, 4, 8, 3, 128], P('gz', 'gy', 'gx'), may hold values from -1 to 1
- wt_patch: int32 [32, 4, 4, 8, 1], P('gz', 'gy', 'gx'), may hold values from 0 to 31; in each aligned block of 8 rows (0 to 7, 8 to 15, ..., all dimensions but the last counted through in order) at most 2 rows name the same one
- patch_coef: float32 [32, 10, 8, 64], P('gz'), may hold values from -0.75 to 0.75
- sph_points: int32 [65536], P(('gx', 'gy', 'gz')), may hold values from 0 to 65535, each once
- sph_cells: int32 [3, 65536], P(None, ('gx', 'gy', 'gz')), may hold values from 1 to 130, as said below
- sph_frac: float32 [3, 65536], P(None, ('gx', 'gy', 'gz')), may hold values from 0 to 1
Outputs:
- section_h: float32 [10, 128, 32, 512], P(None, 'gz', 'gy', 'gx')
- section_p: float32 [10, 128, 32, 512], P(None, 'gz', 'gy', 'gx')
- modes: float32 [32, 10, 961], P('gz')
The draws below stay inside these ranges and needn't reach their ends.
Inputs may be any that keep to these rules, and one draw needn't show every extreme that they name: `wt_patch`: among the blocks of one device at most 2 name the same patch, and in some device exactly 2 do. `wt_cells`: cells are numbered (z * 8 + y) * 128 + x within the device's own block. `sph_points`: every sphere point s * 2048 + r appears exactly once. `sph_cells`: rows are z, y, x indices into the device's block extended by two cells on each side, counted from the outer edge of the extension; row z lies in 1 to 6, row y in 1 to 10, row x in 1 to 130.
All inputs are finite; a program needn't handle non-finite values.
Results may differ from the reference program's by a relative error of at most 0.0041.
Values may be sent and summed in bfloat16 or wider, within the bound.
No kernel may reach another device: no remote copies, remote signals or barrier semaphores. Data moves between devices by JAX's collectives and lax.ppermute only.
A program may use at most 64 MiB of HBM per device.

```python
import math
import jax
import jax.numpy as jnp
import numpy as np
from jax import lax

COMP = 10
CZ = 4
CY = 8
CX = 128
CHEB = 8
BLK = 128
WT_SLOTS = 8
NSPH = 32
LMAX = 30
NTHETA = 32
NPHI = 64
NZ = 128
NY = 32
NX = 512
CAP = 2
NANG = 2048
NPTS = 65536
SPH_SLOTS = 128
N_GX = 4
N_GY = 4
N_GZ = 32


def draw_sph_cells(key, part):
    subkeys = jax.random.split(key, 3)
    along_z = jax.random.randint(subkeys[0], (NPTS,), 1, CZ + 3)
    along_y = jax.random.randint(subkeys[1], (NPTS,), 1, CY + 3)
    along_x = jax.random.randint(subkeys[2], (NPTS,), 1, CX + 3)
    return jnp.stack([along_z, along_y, along_x]).astype(jnp.int32)


def touch_ends(drawn, key, smallest, high):
    extent = drawn.shape
    spot = [jax.random.randint(jax.random.fold_in(key, axis), (), 0, extent[axis]) for axis in range(len(extent))]
    drawn = drawn.at[tuple(spot)].set(smallest)
    longest = extent.index(max(extent))
    spot[longest] = (spot[longest] + 1) % extent[longest]
    return drawn.at[tuple(spot)].set(high)


def block_levels(key, extent, shards, low, largest):
    loudness = 1.0
    for dim, shards_of in shards:
        steps = jax.random.uniform(jax.random.fold_in(jax.random.fold_in(key, 6), dim), (shards_of,), jnp.float32, low / len(shards), largest / len(shards))
        loudness = loudness * jnp.repeat(jnp.exp(steps), extent[dim] // shards_of).reshape((-1,) + (1,) * (len(extent) - 1 - dim))
    return loudness


def shared_out(own_key, own, number, rows, count, top, limit, lean):
    sequence = jax.random.permutation(own_key, count)
    packed, ordinary = shares(count, rows * top, limit, lean, True), shares(count, rows * top, limit, lean, False)
    places = jnp.arange(count)

    def named(tallies, offset_by):
        used = int((tallies > 0).sum())
        fixed = max(1, used // 4)
        shifted = fixed + (places - fixed + offset_by * (used - fixed)) % max(1, count - fixed)
        return jnp.zeros((count,), jnp.int32).at[sequence[jnp.where(places < fixed, places, shifted)]].set(jnp.asarray(tallies, jnp.int32))

    tallies = jnp.where(number % 4 == 0, named(packed, number // 4), named(ordinary, number - number // 4 - 1))
    mixed = jax.random.permutation(jax.random.fold_in(own, 3), count)
    giver, sink = mixed[0:count // 2 * 2:2], mixed[1:count // 2 * 2:2]
    margin = jnp.minimum(tallies[giver] - 1, limit - tallies[sink]) // 2
    margin = jnp.where((giver == sequence[0]) | (sink == sequence[0]) | (tallies[sink] == 0), 0, jnp.maximum(margin, 0))
    shifted = jax.random.randint(jax.random.fold_in(own, 4), (count // 2,), 0, 1 << 20) % (margin + 1)
    tallies = tallies.at[giver].add(-shifted).at[sink].add(shifted)
    labels = jnp.searchsorted(jnp.cumsum(tallies), jnp.arange(rows * top), side="right").astype(jnp.int32)
    listing = labels.reshape(top, rows).T
    listing = listing[jax.random.permutation(jax.random.fold_in(own, 1), rows)]
    offset_by = jax.random.randint(jax.random.fold_in(own, 2), (rows, 1), 0, top)
    return jnp.take_along_axis(listing, (jnp.arange(top)[None, :] + offset_by) % top, axis=1)


def shares(amount, total, bound, skew, full):
    portions = [(1 << 20) // math.isqrt(rank ** skew) + 1 for rank in range(1, amount + 1)]
    largest = bound if full else min(bound, max(-(-total // amount), total * portions[0] // sum(portions)))
    least = 1 if total - largest >= amount - 1 else 0
    holding, spare = [largest] + [least] * (amount - 1), total - largest - least * (amount - 1)
    while spare > 0:
        movable = [i for i in range(1, amount) if holding[i] < largest] or [i for i in range(1, amount) if holding[i] < bound]
        whole, budget = sum([portions[i] for i in movable]), spare
        for i in movable:
            addition = min(bound - holding[i], max(1, budget * portions[i] // whole), spare)
            holding[i] = holding[i] + addition
            spare = spare - addition
    return np.array(holding)


def bell_draw(rng, extent, width, limit, cuts=(), held_as=jnp.bfloat16):
    drawn = jax.random.normal(rng, extent, jnp.float32) * width
    if len(cuts) > 0:
        drawn = block_levels(rng, extent, cuts, -0.22, 0.18) * drawn
    return jnp.clip(drawn, min=-limit, max=limit).astype(held_as)


def setup_inputs(seed: int = 0) -> dict:
    splits = jax.random.split(jax.random.key(seed), 12)
    field_h = bell_draw(splits[0], (COMP, NZ, NY, NX), 1.0, 6.0, ((1, 32), (2, 4), (3, 4)), jnp.float32)
    field_p = bell_draw(splits[1], (COMP, NZ, NY, NX), 1.0, 6.0, ((1, 32), (2, 4), (3, 4)), jnp.float32)
    potential = jnp.clip(jnp.exp(math.log(2.5) - 2.3025851 * jax.random.uniform(splits[2], (NZ, NY, NX), jnp.float32) ** block_levels(splits[2], (NZ, NY, NX), ((0, 32), (1, 4), (2, 4)), -0.2, 0.2)), 0.25, 2.5)
    coupling = bell_draw(splits[3], (COMP, COMP), COMP ** -0.5, 2.0, (), jnp.float32)
    wt_cells = touch_ends(jax.random.randint(splits[4], (N_GZ, N_GY, N_GX, WT_SLOTS, BLK), 0, CZ * CY * CX), jax.random.fold_in(splits[4], 1), 0, (CZ * CY * CX) - 1).astype(jnp.int32)
    wt_coords = jnp.clip(jax.random.uniform(splits[5], (N_GZ, N_GY, N_GX, WT_SLOTS, 3, BLK), jnp.float32, -1.0, 1.0) * block_levels(splits[5], (N_GZ, N_GY, N_GX, WT_SLOTS, 3, BLK), ((0, 32), (1, 4), (2, 4)), -0.4, 0.0), -1.0, 1.0)
    wt_patch_keys = jax.random.split(jax.random.fold_in(splits[6], 1), N_GZ * N_GY * N_GX * WT_SLOTS // WT_SLOTS)
    wt_patch_turns = jax.random.permutation(jax.random.fold_in(splits[6], 3), N_GZ * N_GY * N_GX * WT_SLOTS // WT_SLOTS)
    wt_patch = jax.vmap(lambda own, number: shared_out(jax.random.fold_in(splits[6], 2), own, number, WT_SLOTS, N_GZ, 1, CAP, 2))(wt_patch_keys, wt_patch_turns).reshape((N_GZ, N_GY, N_GX, WT_SLOTS, 1))
    patch_coef = bell_draw(splits[7], (N_GZ, COMP, CHEB, CHEB * CHEB), (CHEB * CHEB * CHEB // 8) ** -0.5, 0.75, ((0, 32),), jnp.float32)
    sph_points = jax.random.permutation(splits[8], NPTS).astype(jnp.int32)
    sph_cells = draw_sph_cells(jax.random.fold_in(splits[11], 71), 0)
    sph_frac = jnp.clip(1.0 * jax.random.uniform(splits[10], (3, NPTS), jnp.float32) ** block_levels(splits[10], (3, NPTS), ((1, 512),), -0.2, 0.2), 0.0, 1.0)
    return dict(field_h=field_h, field_p=field_p, potential=potential, coupling=coupling, wt_cells=wt_cells, wt_coords=wt_coords, wt_patch=wt_patch, patch_coef=patch_coef, sph_points=sph_points, sph_cells=sph_cells, sph_frac=sph_frac)


HALF_STEP = 0.125

def harmonic_table(degree_max, polar_count, azimuth_count):
    polar_angle = np.pi * (np.arange(polar_count) + 0.5) / polar_count
    azimuth = 2.0 * np.pi * np.arange(azimuth_count) / azimuth_count
    cosine = np.cos(polar_angle)
    sine_polar = np.sin(polar_angle)
    legendre = np.zeros((degree_max + 1, degree_max + 1, polar_count))
    diagonal_term = np.full(polar_count, np.sqrt(0.25 / np.pi))
    for order_m in range(degree_max + 1):
        if order_m > 0:
            diagonal_term = diagonal_term * sine_polar * np.sqrt((2.0 * order_m + 1.0) / (2.0 * order_m))
        legendre[order_m, order_m] = diagonal_term
        if order_m < degree_max:
            legendre[order_m + 1, order_m] = cosine * np.sqrt(2.0 * order_m + 3.0) * diagonal_term
        for degree_l in range(order_m + 2, degree_max + 1):
            factor_a = np.sqrt((4.0 * degree_l * degree_l - 1.0) / (degree_l * degree_l - order_m * order_m))
            factor_b = np.sqrt(((degree_l - 1.0) ** 2 - order_m * order_m) / (4.0 * (degree_l - 1.0) ** 2 - 1.0))
            legendre[degree_l, order_m] = factor_a * (cosine * legendre[degree_l - 1, order_m] - factor_b * legendre[degree_l - 2, order_m])
    columns = np.zeros((polar_count, azimuth_count, (degree_max + 1) ** 2))
    weight = sine_polar * np.pi / polar_count
    for degree_l in range(degree_max + 1):
        for order_m in range(-degree_l, degree_l + 1):
            radial = legendre[degree_l, abs(order_m)] * weight
            if order_m == 0:
                angular = np.ones(azimuth_count)
            elif order_m > 0:
                angular = np.sqrt(2.0) * np.cos(order_m * azimuth)
            else:
                angular = np.sqrt(2.0) * np.sin(-order_m * azimuth)
            columns[:, :, degree_l * degree_l + degree_l + order_m] = radial[:, None] * angular[None, :]
    flat_table = columns.reshape(polar_count * azimuth_count, -1).astype(np.float32)
    return jnp.asarray(flat_table).astype(jnp.bfloat16)

def chebyshev(values, terms):
    series = [jnp.ones_like(values), values]
    for index_k in range(2, terms):
        series.append(2.0 * values * series[-1] - series[-2])
    return jnp.stack(series[:terms])

def evaluate(coefficients, positions):
    terms = coefficients.shape[1]
    first = chebyshev(positions[0], terms)
    second = chebyshev(positions[1], terms)
    third = chebyshev(positions[2], terms)
    product = (second[:, None, :] * third[None, :, :]).reshape(terms * terms, -1)
    partial_sum = jnp.dot(coefficients.reshape(-1, terms * terms), product, precision=lax.Precision.HIGHEST, preferred_element_type=jnp.float32)
    partial_sum = partial_sum.reshape(coefficients.shape[0], terms, -1)
    return jnp.einsum('aip,ip->ap', partial_sum, first, precision=lax.Precision.HIGHEST)

def laplace(padded):
    centre = padded[..., 2:-2, 2:-2, 2:-2]
    along_z = -padded[..., 4:, 2:-2, 2:-2] + 16.0 * padded[..., 3:-1, 2:-2, 2:-2] + 16.0 * padded[..., 1:-3, 2:-2, 2:-2] - padded[..., :-4, 2:-2, 2:-2]
    along_y = -padded[..., 2:-2, 4:, 2:-2] + 16.0 * padded[..., 2:-2, 3:-1, 2:-2] + 16.0 * padded[..., 2:-2, 1:-3, 2:-2] - padded[..., 2:-2, :-4, 2:-2]
    along_x = -padded[..., 2:-2, 2:-2, 4:] + 16.0 * padded[..., 2:-2, 2:-2, 3:-1] + 16.0 * padded[..., 2:-2, 2:-2, 1:-3] - padded[..., 2:-2, 2:-2, :-4]
    return (along_z + along_y + along_x - 90.0 * centre) / 12.0

def trilinear(flat_field, span_y, span_x, corner, fraction):
    summed = jnp.zeros((flat_field.shape[0], corner.shape[1]), jnp.float32)
    for step_z in (0, 1):
        weight_z = fraction[0] if step_z else 1.0 - fraction[0]
        for step_y in (0, 1):
            weight_y = fraction[1] if step_y else 1.0 - fraction[1]
            for step_x in (0, 1):
                weight_x = fraction[2] if step_x else 1.0 - fraction[2]
                position = ((corner[0] + step_z) * span_y + corner[1] + step_y) * span_x + corner[2] + step_x
                summed = summed + (weight_z * weight_y * weight_x)[None, :] * jnp.take(flat_field, position, axis=1)
    return summed

def reference(field_h, field_p, potential, coupling, wt_cells, wt_coords, wt_patch, patch_coef, sph_points, sph_cells, sph_frac):
    laplacian = lax.map(lambda component: laplace(jnp.pad(component, 2)), field_h)
    coupled = jnp.einsum('ab,bzyx->azyx', coupling, field_h, precision=lax.Precision.HIGHEST)
    right_side = laplacian - potential[None] * coupled
    device_total = N_GZ * N_GY * N_GX
    positions = wt_coords.reshape(device_total, WT_SLOTS, 3, BLK)
    patch_ids = wt_patch.reshape(device_total, WT_SLOTS)

    def per_device(block_item):
        return jax.vmap(evaluate)(patch_coef[block_item[1]], block_item[0])
    source = lax.map(per_device, (positions, patch_ids))
    device_index = jnp.arange(device_total, dtype=jnp.int32)
    index_z = device_index // (N_GY * N_GX)
    index_y = device_index // N_GX % N_GY
    index_x = device_index % N_GX
    cell_ids = wt_cells.reshape(device_total, WT_SLOTS * BLK)
    global_z = (index_z[:, None] * CZ + cell_ids // (CY * CX)).reshape(-1)
    global_y = (index_y[:, None] * CY + cell_ids // CX % CY).reshape(-1)
    global_x = (index_x[:, None] * CX + cell_ids % CX).reshape(-1)
    spread = jnp.moveaxis(source, 2, 0).reshape(COMP, -1)
    right_side = right_side.at[:, global_z, global_y, global_x].add(spread)
    section_h = field_h + HALF_STEP * field_p
    section_p = field_p + HALF_STEP * right_side
    padded = jnp.pad(field_h, ((0, 0), (2, 2), (2, 2), (2, 2)))
    flat_field = padded.reshape(COMP, -1)
    slot_index = jnp.arange(NPTS, dtype=jnp.int32)
    owner = slot_index // SPH_SLOTS
    owner_x = owner // (N_GY * N_GZ)
    owner_y = owner // N_GZ % N_GY
    owner_z = owner % N_GZ
    corner = jnp.stack([owner_z * CZ + sph_cells[0], owner_y * CY + sph_cells[1], owner_x * CX + sph_cells[2]])
    point_values = trilinear(flat_field, NY + 4, NX + 4, corner, sph_frac).astype(jnp.bfloat16)
    dense = jnp.zeros((NPTS, COMP), jnp.bfloat16).at[sph_points].set(point_values.T)
    coef_table = harmonic_table(LMAX, NTHETA, NPHI)
    modes = jnp.einsum('sac,am->scm', dense.reshape(NSPH, NANG, COMP).astype(jnp.float32), coef_table.astype(jnp.float32), precision=lax.Precision.HIGHEST)
    return (section_h, section_p, modes)
```

```python
import functools

import jax
import jax.numpy as jnp
import numpy as np
from jax import lax
from jax.experimental import pallas as pl
from jax.experimental.pallas import tpu as pltpu
from jax.sharding import PartitionSpec as P

LMAX = 30
NTHETA = 32
NPHI = 64
NANG = NTHETA * NPHI
NMODE = (LMAX + 1) ** 2
HALF_STEP = 0.125

COMP = 10
CZ = 4
CY = 8
CX = 128
LANES = 128
ROWS_OWN = COMP * CZ * CY
ROWS_SLAB = COMP * 2 * CY
ROWS_ALL = ROWS_OWN + 4 * ROWS_SLAB
MODE_TILES = 8
MODE_ROWS = COMP * MODE_TILES
CHEB = 8
COEF_ROWS = COMP * CHEB * CHEB * CHEB // LANES
POINT_ROWS = 16
SLOTS = 8

F32 = jnp.float32
BF16 = jnp.bfloat16
HIGHEST = lax.Precision.HIGHEST
NN = (((1,), (0,)), ((), ()))
NT = (((1,), (1,)), ((), ()))
TN = (((0,), (0,)), ((), ()))


def mode_factors():
    polar = np.pi * (np.arange(NTHETA) + 0.5) / NTHETA
    azimuth = 2.0 * np.pi * np.arange(NPHI) / NPHI
    cosine, sine = np.cos(polar), np.sin(polar)
    legendre = np.zeros((LMAX + 1, LMAX + 1, NTHETA))
    diagonal = np.full(NTHETA, np.sqrt(0.25 / np.pi))
    for m in range(LMAX + 1):
        if m > 0:
            diagonal = diagonal * sine * np.sqrt((2.0 * m + 1.0) / (2.0 * m))
        legendre[m, m] = diagonal
        if m < LMAX:
            legendre[m + 1, m] = cosine * np.sqrt(2.0 * m + 3.0) * diagonal
        for l in range(m + 2, LMAX + 1):
            a = np.sqrt((4.0 * l * l - 1.0) / (l * l - m * m))
            b = np.sqrt(((l - 1.0) ** 2 - m * m) / (4.0 * (l - 1.0) ** 2 - 1.0))
            legendre[l, m] = a * (cosine * legendre[l - 1, m] - b * legendre[l - 2, m])
    width = MODE_TILES * LANES
    radial = np.zeros((NTHETA, width))
    angular = np.zeros((NPHI, width))
    weight = sine * np.pi / NTHETA
    for l in range(LMAX + 1):
        for m in range(-l, l + 1):
            n = l * l + l + m
            radial[:, n] = legendre[l, abs(m)] * weight
            if m == 0:
                angular[:, n] = 1.0
            elif m > 0:
                angular[:, n] = np.sqrt(2.0) * np.cos(m * azimuth)
            else:
                angular[:, n] = np.sqrt(2.0) * np.sin(-m * azimuth)
    angular = angular.astype(np.float32)
    high = angular.astype(jnp.bfloat16)
    low = (angular - high.astype(np.float32)).astype(jnp.bfloat16)
    return radial.astype(np.float32), np.concatenate([high, low], axis=0)


def iota(shape, dim):
    return lax.broadcasted_iota(jnp.int32, shape, dim)


def split2(value):
    high = value.astype(BF16)
    return high, (value - high.astype(F32)).astype(BF16)


def dot(a, b, dims, precision=None):
    return lax.dot_general(a, b, dims, precision=precision, preferred_element_type=F32)


def two_hot(position, cell, fraction):
    return jnp.where(position == cell, 1.0 - fraction, 0.0) + jnp.where(
        position == cell + 1, fraction, 0.0
    )


def weighted_rows(parts, cells, frac):
    own, zl, zh, yl, yh = parts
    lane8 = iota((8, LANES), 0)
    row16 = iota((16, LANES), 0)
    wy = two_hot(lane8 + 2, cells[1:2], frac[1:2])
    plane = [two_hot(z, cells[0:1], frac[0:1]) * wy for z in range(CZ + 4)]
    wz16 = two_hot(row16 // 2, cells[0:1], frac[0:1])
    wyl = wz16 * two_hot(row16 % 2, cells[1:2], frac[1:2])
    wyh = wz16 * two_hot(row16 % 2 + CY + 2, cells[1:2], frac[1:2])
    rows = []
    for c in range(COMP):
        total = jnp.zeros((8, LANES), F32)
        for z in range(CZ):
            base = (c * CZ + z) * CY
            total += own[base : base + 8] * plane[z + 2]
        for z in range(2):
            base = (c * 2 + z) * CY
            total += zl[base : base + 8] * plane[z]
            total += zh[base : base + 8] * plane[z + 6]
            base = c * 16 + z * 8
            total += yl[base : base + 8] * wyl[z * 8 : z * 8 + 8]
            total += yh[base : base + 8] * wyh[z * 8 : z * 8 + 8]
        rows.append(jnp.sum(total, axis=0, keepdims=True))
    return jnp.concatenate(rows, axis=0)


def y_slab_kernel(h, zl, zh, first, last):
    for c in range(COMP):
        for z in range(CZ + 4):
            source = zl.at[c, z] if z < 2 else h.at[c, z - 2] if z < CZ + 2 else zh.at[c, z - CZ - 2]
            row = (c * (CZ + 4) + z) * 2
            first[row : row + 2, :] = source[0:2, :]
            last[row : row + 2, :] = source[CY - 2 : CY, :]


def all_rows(h, zl, zh, yl, yh):
    return (
        h[...].reshape(ROWS_OWN, LANES),
        zl[...].reshape(ROWS_SLAB, LANES),
        zh[...].reshape(ROWS_SLAB, LANES),
        yl[...],
        yh[...],
    )


def x_edge_kernel(h, zl, zh, yl, yh, first, last):
    row = iota((8, LANES), 0)
    lane = iota((8, LANES), 1)
    place = jnp.where(row < 2, row, row + CX - 4)
    pick = jnp.where(lane == place, 1.0, 0.0).astype(BF16)
    at = 0
    for part in all_rows(h, zl, zh, yl, yh):
        high, low = split2(part)
        edge = dot(pick, high, NT) + dot(pick, low, NT)
        size = part.shape[0]
        first[:, at : at + size] = edge[0:2]
        last[:, at : at + size] = edge[2:4]
        at += size


def interior_points_kernel(h, zl, zh, yl, yh, cells, frac, out):
    cell, fraction = cells[...], frac[...]
    wx = two_hot(iota((CX, LANES), 0) + 2, cell[2:3], fraction[2:3])
    parts = [dot(part, wx, NN, HIGHEST) for part in all_rows(h, zl, zh, yl, yh)]
    out[...] = weighted_rows(parts, cell, fraction)


def pack_kernel(inner, xl, xr, cells, frac, points, coef, out):
    cell, fraction = cells[...], frac[...]
    edges = jnp.concatenate([xl[...], xr[...]], axis=0)
    place = iota((4, LANES), 0)
    place = jnp.where(place < 2, place, place + CX)
    wx = two_hot(place, cell[2:3], fraction[2:3])
    grown = dot(edges, wx, TN, HIGHEST)
    cuts = (0, 320, 480, 640, 800, 960)
    parts = [grown[a:b] for a, b in zip(cuts[:-1], cuts[1:])]
    values = inner[...] + weighted_rows(parts, cell, fraction)
    point = points[...]
    sphere = point // NANG
    polar = (point // NPHI % NTHETA).astype(F32)
    azimuth = (point % NPHI).astype(F32)
    tail = jnp.zeros((POINT_ROWS - COMP - 2, LANES), F32)
    coefficients = coef[...].astype(BF16)
    for s in range(out.shape[0]):
        node = jnp.where(sphere == s, polar, 255.0)
        block = jnp.concatenate([values, node, azimuth, tail], axis=0)
        out[s, 0:POINT_ROWS, :] = block.astype(BF16)
        out[s, POINT_ROWS : POINT_ROWS + COEF_ROWS, :] = coefficients


def partial_modes_kernel(arrived, radial, angular, out, rows):
    row_i = iota((NTHETA, LANES), 0).astype(F32)
    row_j = iota((NPHI, LANES), 0).astype(F32)
    dense = jnp.zeros((COMP * NTHETA, NPHI), F32)
    for s in range(0, arrived.shape[0], 2):
        left, right = [], []
        for k in (s, s + 1):
            block = arrived[k, 0:POINT_ROWS, :].astype(F32)
            at_i = row_i == block[COMP : COMP + 1]
            at_j = row_j == block[COMP + 1 : COMP + 2]
            left.append(
                jnp.concatenate(
                    [jnp.where(at_i, block[c : c + 1], 0.0) for c in range(COMP)], axis=0
                ).astype(BF16)
            )
            right.append(jnp.where(at_j, 1.0, 0.0).astype(BF16))
        dense += dot(
            jnp.concatenate(left, axis=1), jnp.concatenate(right, axis=1), NT
        )
    exact = dense.astype(BF16)
    exact = jnp.concatenate([exact, exact], axis=1)
    for t in range(MODE_TILES):
        lanes = slice(t * LANES, (t + 1) * LANES)
        grown = dot(exact, angular[:, lanes], NN)
        weight = radial[:, lanes]
        for c in range(COMP):
            part = grown[c * NTHETA : (c + 1) * NTHETA] * weight
            rows[t * COMP + c : t * COMP + c + 1, :] = jnp.sum(part, axis=0, keepdims=True)
    sent = rows[...].astype(BF16)
    for k in range(out.shape[0]):
        out[k] = sent


def sum_modes_kernel(arrived, out):
    total = arrived[0].astype(F32)
    for k in range(1, arrived.shape[0]):
        total += arrived[k].astype(F32)
    for t in range(MODE_TILES):
        width = min(LANES, NMODE - t * LANES)
        for c in range(COMP):
            row = t * COMP + c
            out[c, :, t * LANES : t * LANES + width] = total[row : row + 1, :width]


def right_side_kernel(h, zl, zh, yl, yh, p, potential, coupling, section_h, out):
    row = iota((CY, LANES), 0)
    lane = iota((CY, LANES), 1)
    for c in range(COMP):
        layers = [zl[c, 0], zl[c, 1]] + [h[c, z] for z in range(CZ)] + [zh[c, 0], zh[c, 1]]
        for z in range(CZ):
            mid = layers[z + 2]
            along_z = 16.0 * (layers[z + 1] + layers[z + 3]) - (layers[z] + layers[z + 4])
            at = (c * (CZ + 4) + z + 2) * 2
            above, below = yh[at : at + 2, :], yl[at : at + 2, :]
            ring = jnp.concatenate([above, mid[2:6], below], axis=0)
            y1 = pltpu.roll(jnp.where(row == 0, ring, mid), CY - 1, 0)
            y2 = pltpu.roll(jnp.where(row < 2, ring, mid), CY - 2, 0)
            m1 = pltpu.roll(jnp.where(row == CY - 1, ring, mid), 1, 0)
            m2 = pltpu.roll(jnp.where(row >= CY - 2, ring, mid), 2, 0)
            along_y = 16.0 * (y1 + m1) - (y2 + m2)
            x1 = jnp.where(lane < CX - 1, pltpu.roll(mid, CX - 1, 1), 0.0)
            x2 = jnp.where(lane < CX - 2, pltpu.roll(mid, CX - 2, 1), 0.0)
            n1 = jnp.where(lane >= 1, pltpu.roll(mid, 1, 1), 0.0)
            n2 = jnp.where(lane >= 2, pltpu.roll(mid, 2, 1), 0.0)
            along_x = 16.0 * (x1 + n1) - (x2 + n2)
            laplacian = (along_z + along_y + along_x - 90.0 * mid) * (1.0 / 12.0)
            coupled = coupling[c, 0] * h[0, z]
            for b in range(1, COMP):
                coupled += coupling[c, b] * h[b, z]
            momentum = p[c, z]
            section_h[c, z] = mid + HALF_STEP * momentum
            out[c, z] = momentum + HALF_STEP * (laplacian - potential[z] * coupled)


def source_kernel(patch, arrived, coords, cells, partial, xl, xr, out, series, terms, sources):
    for axis in range(3):
        value = coords[axis]
        older, newer = jnp.ones_like(value), value
        for n in range(CHEB):
            series[axis, n * SLOTS : (n + 1) * SLOTS, :] = older
            older, newer = newer, 2.0 * value * newer - older
    for slot in range(SLOTS):
        third = series[2, pl.ds(slot, CHEB, stride=SLOTS), :]
        product = jnp.concatenate(
            [series[1, n * SLOTS + slot : n * SLOTS + slot + 1, :] * third for n in range(CHEB)],
            axis=0,
        )
        high, low = split2(product)
        empty = jnp.zeros((CHEB * CHEB, LANES), BF16)
        block = arrived[patch[slot], POINT_ROWS : POINT_ROWS + COEF_ROWS, :]
        grown = jnp.zeros((COEF_ROWS, 2 * LANES), F32)
        for part in (high, low):
            wide = jnp.concatenate(
                [jnp.concatenate([part, empty], axis=0), jnp.concatenate([empty, part], axis=0)],
                axis=1,
            )
            grown += dot(block, wide, NN)
        even = series[0, pl.ds(slot, 4, stride=2 * SLOTS), :]
        odd = series[0, pl.ds(slot + SLOTS, 4, stride=2 * SLOTS), :]
        even = jnp.concatenate([even] * COMP, axis=0)
        odd = jnp.concatenate([odd] * COMP, axis=0)
        terms[slot * COEF_ROWS : (slot + 1) * COEF_ROWS, :] = (
            grown[:, :LANES] * even + grown[:, LANES:] * odd
        )
    count = SLOTS * COMP
    total = terms[pl.ds(0, count, stride=4), :]
    for m in range(1, 4):
        total += terms[pl.ds(m, count, stride=4), :]
    sources[...] = total
    cell = cells[...]
    layer, column = cell // CX, cell % CX
    row_l = iota((CZ * CY, LANES), 0)
    row_x = iota((CX, LANES), 0)
    added = jnp.zeros((ROWS_OWN, CX), F32)
    for slot in range(0, SLOTS, 2):
        left, right = [], []
        for k in (slot, slot + 1):
            at_l = row_l == layer[k : k + 1]
            at_x = row_x == column[k : k + 1]
            left.append(
                jnp.concatenate(
                    [
                        jnp.where(at_l, sources[k * COMP + c : k * COMP + c + 1, :], 0.0)
                        for c in range(COMP)
                    ],
                    axis=0,
                ).astype(BF16)
            )
            right.append(jnp.where(at_x, 1.0, 0.0).astype(BF16))
        added += dot(jnp.concatenate(left, axis=1), jnp.concatenate(right, axis=1), NT)
    edges = jnp.concatenate([xl[:, :ROWS_OWN], xr[:, :ROWS_OWN]], axis=0)
    place = iota((4, LANES), 0)
    place = jnp.where(place < 2, place - 2, place + CX - 2)
    far = jnp.abs(place - iota((4, LANES), 1))
    stencil = jnp.where(far == 1, 16.0, jnp.where(far == 2, -1.0, 0.0))
    added += dot(edges, stencil, TN, HIGHEST) * (1.0 / 12.0)
    out[...] = partial[...] + HALF_STEP * added.reshape(COMP, CZ, CY, CX)


def call(kernel, outs, scratch=(), smem=(), count=0):
    specs = [
        pl.BlockSpec(memory_space=pltpu.SMEM if k in smem else pltpu.VMEM) for k in range(count)
    ]
    return pl.pallas_call(
        kernel,
        out_shape=outs,
        in_specs=specs,
        scratch_shapes=scratch,
        name=kernel.__name__,
    )


def shape(dims, dtype=F32):
    return jax.ShapeDtypeStruct(dims, dtype)


def neighbours(axis):
    count = lax.axis_size(axis)
    forward = [(i, i + 1) for i in range(count - 1)]
    return forward, [(b, a) for a, b in forward]


def shards(
    field_h,
    field_p,
    potential,
    coupling,
    wt_cells,
    wt_coords,
    wt_patch,
    patch_coef,
    sph_points,
    sph_cells,
    sph_frac,
):
    z_count = lax.axis_size("gz")
    xy_count = lax.axis_size("gx") * lax.axis_size("gy")
    up, down = neighbours("gz")
    zl = lax.ppermute(field_h[:, CZ - 2 :], "gz", up)
    zh = lax.ppermute(field_h[:, :2], "gz", down)
    slab = shape((ROWS_SLAB, LANES))
    first, last = call(y_slab_kernel, (slab, slab), count=3)(field_h, zl, zh)
    up, down = neighbours("gy")
    yl = lax.ppermute(last, "gy", up)
    yh = lax.ppermute(first, "gy", down)
    grid = (field_h, zl, zh, yl, yh)
    edge = shape((2, ROWS_ALL))
    first, last = call(x_edge_kernel, (edge, edge), count=5)(*grid)
    up, down = neighbours("gx")
    xl = lax.ppermute(last, "gx", up)
    xr = lax.ppermute(first, "gx", down)
    inner = call(interior_points_kernel, shape((COMP, LANES)), count=7)(
        *grid, sph_cells, sph_frac
    )
    cube = shape((COMP, CZ, CY, CX))
    section_h, partial = call(right_side_kernel, (cube, cube), count=8, smem=(7,))(
        *grid, field_p, potential, coupling
    )
    packed = call(
        pack_kernel, shape((z_count, POINT_ROWS + COEF_ROWS, LANES), BF16), count=7
    )(
        inner,
        xl,
        xr,
        sph_cells,
        sph_frac,
        sph_points.reshape(1, LANES),
        patch_coef.reshape(COEF_ROWS, LANES),
    )
    arrived = lax.all_to_all(packed, "gz", 0, 0, tiled=True)
    radial, angular = mode_factors()
    sent = call(
        partial_modes_kernel,
        shape((xy_count, MODE_ROWS, LANES), BF16),
        scratch=[pltpu.VMEM((MODE_ROWS, LANES), F32)],
        count=3,
    )(arrived, jnp.asarray(radial), jnp.asarray(angular))
    gathered = lax.all_to_all(sent, ("gx", "gy"), 0, 0, tiled=True)
    section_p = call(
        source_kernel,
        cube,
        scratch=[
            pltpu.VMEM((3, CHEB * SLOTS, LANES), F32),
            pltpu.VMEM((SLOTS * COEF_ROWS, LANES), F32),
            pltpu.VMEM((SLOTS * COMP, LANES), F32),
        ],
        count=7,
        smem=(0,),
    )(
        wt_patch.reshape(SLOTS),
        arrived,
        jnp.moveaxis(wt_coords[0, 0, 0], 1, 0),
        wt_cells[0, 0, 0],
        partial,
        xl,
        xr,
    )
    modes = call(sum_modes_kernel, shape((COMP, 1, NMODE)), count=1)(gathered)
    return section_h, section_p, jnp.moveaxis(modes, 1, 0)


def solution(mesh):
    placed = (
        P(None, "gz", "gy", "gx"),
        P(None, "gz", "gy", "gx"),
        P("gz", "gy", "gx"),
        P(),
        P("gz", "gy", "gx", None, None),
        P("gz", "gy", "gx", None, None, None),
        P("gz", "gy", "gx", None, None),
        P("gz", None, None, None),
        P(("gx", "gy", "gz")),
        P(None, ("gx", "gy", "gz")),
        P(None, ("gx", "gy", "gz")),
    )
    return jax.shard_map(
        shards,
        mesh=mesh,
        in_specs=placed,
        out_specs=(P(None, "gz", "gy", "gx"), P(None, "gz", "gy", "gx"), P("gz", None, None)),
        check_vma=False,
    )
```

```python
import functools

import jax
import jax.numpy as jnp
import numpy as np
from jax import lax
from jax.experimental import pallas as pl
from jax.experimental.pallas import tpu as pltpu
from jax.sharding import PartitionSpec as P

LMAX = 30
NTHETA = 32
NPHI = 64
NANG = NTHETA * NPHI
NMODE = (LMAX + 1) ** 2
HALF_STEP = 0.125

COMP = 10
CZ = 4
CY = 8
CX = 128
LANES = 128
ROWS_OWN = COMP * CZ * CY
ROWS_SLAB = COMP * 2 * CY
ROWS_ALL = ROWS_OWN + 4 * ROWS_SLAB
MODE_TILES = 8
MODE_ROWS = COMP * MODE_TILES
CHEB = 8
HALF = COMP // 2
POINT_ROWS = COMP + 2
SENT_ROWS = 32
SLOTS = 8
VMEM_GRANT = 8 << 20

F32 = jnp.float32
BF16 = jnp.bfloat16
HIGHEST = lax.Precision.HIGHEST
NN = (((1,), (0,)), ((), ()))
NT = (((1,), (1,)), ((), ()))
TN = (((0,), (0,)), ((), ()))


def mode_factors():
    polar = np.pi * (np.arange(NTHETA) + 0.5) / NTHETA
    azimuth = 2.0 * np.pi * np.arange(NPHI) / NPHI
    cosine, sine = np.cos(polar), np.sin(polar)
    legendre = np.zeros((LMAX + 1, LMAX + 1, NTHETA))
    diagonal = np.full(NTHETA, np.sqrt(0.25 / np.pi))
    for m in range(LMAX + 1):
        if m > 0:
            diagonal = diagonal * sine * np.sqrt((2.0 * m + 1.0) / (2.0 * m))
        legendre[m, m] = diagonal
        if m < LMAX:
            legendre[m + 1, m] = cosine * np.sqrt(2.0 * m + 3.0) * diagonal
        for l in range(m + 2, LMAX + 1):
            a = np.sqrt((4.0 * l * l - 1.0) / (l * l - m * m))
            b = np.sqrt(((l - 1.0) ** 2 - m * m) / (4.0 * (l - 1.0) ** 2 - 1.0))
            legendre[l, m] = a * (cosine * legendre[l - 1, m] - b * legendre[l - 2, m])
    width = MODE_TILES * LANES
    radial = np.zeros((NTHETA, width))
    angular = np.zeros((NPHI, width))
    weight = sine * np.pi / NTHETA
    for l in range(LMAX + 1):
        for m in range(-l, l + 1):
            n = l * l + l + m
            radial[:, n] = legendre[l, abs(m)] * weight
            if m == 0:
                angular[:, n] = 1.0
            elif m > 0:
                angular[:, n] = np.sqrt(2.0) * np.cos(m * azimuth)
            else:
                angular[:, n] = np.sqrt(2.0) * np.sin(-m * azimuth)
    angular = angular.astype(np.float32)
    high = angular.astype(jnp.bfloat16)
    low = (angular - high.astype(np.float32)).astype(jnp.bfloat16)
    return radial.astype(np.float32), np.concatenate([high, low], axis=0)


def iota(shape, dim):
    return lax.broadcasted_iota(jnp.int32, shape, dim)


def split2(value):
    high = value.astype(BF16)
    return high, (value - high.astype(F32)).astype(BF16)


def dot(a, b, dims, precision=None):
    return lax.dot_general(a, b, dims, precision=precision, preferred_element_type=F32)


def two_hot(position, cell, fraction):
    return jnp.where(position == cell, 1.0 - fraction, 0.0) + jnp.where(
        position == cell + 1, fraction, 0.0
    )


def weighted_rows(parts, cells, frac):
    own, zl, zh, yl, yh = parts
    lane8 = iota((8, LANES), 0)
    row16 = iota((16, LANES), 0)
    wy = two_hot(lane8 + 2, cells[1:2], frac[1:2])
    plane = [two_hot(z, cells[0:1], frac[0:1]) * wy for z in range(CZ + 4)]
    wz16 = two_hot(row16 // 2, cells[0:1], frac[0:1])
    wyl = wz16 * two_hot(row16 % 2, cells[1:2], frac[1:2])
    wyh = wz16 * two_hot(row16 % 2 + CY + 2, cells[1:2], frac[1:2])
    rows = []
    for c in range(COMP):
        total = jnp.zeros((8, LANES), F32)
        for z in range(CZ):
            base = (c * CZ + z) * CY
            total += own[base : base + 8] * plane[z + 2]
        for z in range(2):
            base = (c * 2 + z) * CY
            total += zl[base : base + 8] * plane[z]
            total += zh[base : base + 8] * plane[z + 6]
            base = c * 16 + z * 8
            total += yl[base : base + 8] * wyl[z * 8 : z * 8 + 8]
            total += yh[base : base + 8] * wyh[z * 8 : z * 8 + 8]
        rows.append(jnp.sum(total, axis=0, keepdims=True))
    return jnp.concatenate(rows, axis=0)


def y_slab_kernel(h, zl, zh, first, last):
    for c in range(COMP):
        for z in range(CZ + 4):
            source = zl.at[c, z] if z < 2 else h.at[c, z - 2] if z < CZ + 2 else zh.at[c, z - CZ - 2]
            row = (c * (CZ + 4) + z) * 2
            first[row : row + 2, :] = source[0:2, :]
            last[row : row + 2, :] = source[CY - 2 : CY, :]


def all_rows(h, zl, zh, yl, yh):
    return (
        h[...].reshape(ROWS_OWN, LANES),
        zl[...].reshape(ROWS_SLAB, LANES),
        zh[...].reshape(ROWS_SLAB, LANES),
        yl[...],
        yh[...],
    )


def x_edge_kernel(h, zl, zh, yl, yh, first, last):
    row = iota((8, LANES), 0)
    lane = iota((8, LANES), 1)
    place = jnp.where(row < 2, row, row + CX - 4)
    pick = jnp.where(lane == place, 1.0, 0.0).astype(BF16)
    at = 0
    for part in all_rows(h, zl, zh, yl, yh):
        high, low = split2(part)
        edge = dot(pick, high, NT) + dot(pick, low, NT)
        size = part.shape[0]
        first[:, at : at + size] = edge[0:2]
        last[:, at : at + size] = edge[2:4]
        at += size


def interior_points_kernel(h, zl, zh, yl, yh, cells, frac, out):
    cell, fraction = cells[...], frac[...]
    wx = two_hot(iota((CX, LANES), 0) + 2, cell[2:3], fraction[2:3])
    parts = [dot(part, wx, NN, HIGHEST) for part in all_rows(h, zl, zh, yl, yh)]
    out[...] = weighted_rows(parts, cell, fraction)


def pack_kernel(core, inner, xl, xr, cells, frac, points, coef, out):
    cell, fraction = cells[...], frac[...]
    edges = jnp.concatenate([xl[...], xr[...]], axis=0)
    place = iota((4, LANES), 0)
    place = jnp.where(place < 2, place, place + CX)
    wx = two_hot(place, cell[2:3], fraction[2:3])
    grown = dot(edges, wx, TN, HIGHEST)
    cuts = (0, 320, 480, 640, 800, 960)
    parts = [grown[a:b] for a, b in zip(cuts[:-1], cuts[1:])]
    values = inner[...] + weighted_rows(parts, cell, fraction)
    point = points[...]
    sphere = point // NANG
    polar = (point // NPHI % NTHETA).astype(F32)
    azimuth = (point % NPHI).astype(F32)
    quarter = [
        jnp.concatenate(
            [jnp.where(core[0] == 0, coef[c, 0:4, :], coef[c, 4:8, :]) for c in (a, a + HALF)],
            axis=1,
        )
        for a in range(HALF)
    ]
    main = jnp.concatenate(quarter[:4], axis=0).astype(BF16)
    for s in range(out.shape[0]):
        node = jnp.where(sphere == s, polar, 255.0)
        block = jnp.concatenate([values, node, azimuth, quarter[4]], axis=0)
        out[s, 0:16, :] = block.astype(BF16)
        out[s, 16:32, :] = main


def partial_modes_kernel(arrived, radial, angular, out, rows):
    row_i = iota((NTHETA, LANES), 0).astype(F32)
    row_j = iota((NPHI, LANES), 0).astype(F32)
    dense = jnp.zeros((COMP * NTHETA, NPHI), F32)
    for s in range(0, arrived.shape[0], 2):
        left, right = [], []
        for k in (s, s + 1):
            block = arrived[k, 0:16, :].astype(F32)
            at_i = row_i == block[COMP : COMP + 1]
            at_j = row_j == block[COMP + 1 : COMP + 2]
            left.append(
                jnp.concatenate(
                    [jnp.where(at_i, block[c : c + 1], 0.0) for c in range(COMP)], axis=0
                ).astype(BF16)
            )
            right.append(jnp.where(at_j, 1.0, 0.0).astype(BF16))
        dense += dot(
            jnp.concatenate(left, axis=1), jnp.concatenate(right, axis=1), NT
        )
    exact = dense.astype(BF16)
    exact = jnp.concatenate([exact, exact], axis=1)
    for t in range(MODE_TILES):
        lanes = slice(t * LANES, (t + 1) * LANES)
        grown = dot(exact, angular[:, lanes], NN)
        weight = radial[:, lanes]
        for c in range(COMP):
            part = grown[c * NTHETA : (c + 1) * NTHETA] * weight
            rows[t * COMP + c : t * COMP + c + 1, :] = jnp.sum(part, axis=0, keepdims=True)
    sent = rows[...].astype(BF16)
    for k in range(out.shape[0]):
        out[k] = sent


def sum_modes_kernel(arrived, out):
    total = arrived[0].astype(F32)
    for k in range(1, arrived.shape[0]):
        total += arrived[k].astype(F32)
    for t in range(MODE_TILES):
        width = min(LANES, NMODE - t * LANES)
        for c in range(COMP):
            row = t * COMP + c
            out[c, :, t * LANES : t * LANES + width] = total[row : row + 1, :width]


def right_side_kernel(h, zl, zh, yl, yh, p, potential, coupling, section_h, out):
    row = iota((CY, LANES), 0)
    lane = iota((CY, LANES), 1)
    for c in range(COMP):
        layers = [zl[c, 0], zl[c, 1]] + [h[c, z] for z in range(CZ)] + [zh[c, 0], zh[c, 1]]
        for z in range(CZ):
            mid = layers[z + 2]
            along_z = 16.0 * (layers[z + 1] + layers[z + 3]) - (layers[z] + layers[z + 4])
            at = (c * (CZ + 4) + z + 2) * 2
            above, below = yh[at : at + 2, :], yl[at : at + 2, :]
            ring = jnp.concatenate([above, mid[2:6], below], axis=0)
            y1 = pltpu.roll(jnp.where(row == 0, ring, mid), CY - 1, 0)
            y2 = pltpu.roll(jnp.where(row < 2, ring, mid), CY - 2, 0)
            m1 = pltpu.roll(jnp.where(row == CY - 1, ring, mid), 1, 0)
            m2 = pltpu.roll(jnp.where(row >= CY - 2, ring, mid), 2, 0)
            along_y = 16.0 * (y1 + m1) - (y2 + m2)
            x1 = jnp.where(lane < CX - 1, pltpu.roll(mid, CX - 1, 1), 0.0)
            x2 = jnp.where(lane < CX - 2, pltpu.roll(mid, CX - 2, 1), 0.0)
            n1 = jnp.where(lane >= 1, pltpu.roll(mid, 1, 1), 0.0)
            n2 = jnp.where(lane >= 2, pltpu.roll(mid, 2, 1), 0.0)
            along_x = 16.0 * (x1 + n1) - (x2 + n2)
            laplacian = (along_z + along_y + along_x - 90.0 * mid) * (1.0 / 12.0)
            coupled = coupling[c, 0] * h[0, z]
            for b in range(1, COMP):
                coupled += coupling[c, b] * h[b, z]
            momentum = p[c, z]
            section_h[c, z] = mid + HALF_STEP * momentum
            out[c, z] = momentum + HALF_STEP * (laplacian - potential[z] * coupled)


def source_kernel(
    core, patch, mine, other, coords, cells, partial, xl, xr, out, series, terms, sources
):
    for axis in range(3):
        value = coords[axis]
        older, newer = jnp.ones_like(value), value
        for n in range(CHEB):
            series[axis, n * SLOTS : (n + 1) * SLOTS, :] = older
            older, newer = newer, 2.0 * value * newer - older
    for slot in range(SLOTS):
        third = series[2, pl.ds(slot, CHEB, stride=SLOTS), :]
        product = jnp.concatenate(
            [series[1, n * SLOTS + slot : n * SLOTS + slot + 1, :] * third for n in range(CHEB)],
            axis=0,
        )
        high, low = split2(product)
        empty = jnp.zeros((CHEB * CHEB, LANES), BF16)
        chosen = patch[slot]
        first, second = mine[chosen], other[chosen]
        block = jnp.concatenate([first[16:32], second[16:32], first[0:16], second[0:16]], axis=0)
        grown = jnp.zeros((64, 2 * LANES), F32)
        for part in (high, low):
            wide = jnp.concatenate(
                [jnp.concatenate([part, empty], axis=0), jnp.concatenate([empty, part], axis=0)],
                axis=1,
            )
            grown += dot(block, wide, NN)
        start = series[0, pl.ds(slot, 4, stride=SLOTS), :]
        end = series[0, pl.ds(slot + 4 * SLOTS, 4, stride=SLOTS), :]
        near = jnp.where(core[0] == 0, start, end)
        far = jnp.where(core[0] == 0, end, start)
        near, far = jnp.concatenate([near] * 4, axis=0), jnp.concatenate([far] * 4, axis=0)
        for side in range(2):
            lanes = slice(side * LANES, (side + 1) * LANES)
            main = grown[0:16, lanes] * near + grown[16:32, lanes] * far
            rest = grown[44:48, lanes] * near[0:4] + grown[60:64, lanes] * far[0:4]
            row = (slot * 2 + side) * 20
            terms[row : row + 16, :] = main
            terms[row + 16 : row + 20, :] = rest
    count = SLOTS * COMP
    total = terms[pl.ds(0, count, stride=4), :]
    for m in range(1, 4):
        total += terms[pl.ds(m, count, stride=4), :]
    sources[...] = total
    cell = cells[...]
    layer, column = cell // CX, cell % CX
    row_l = iota((CZ * CY, LANES), 0)
    row_x = iota((CX, LANES), 0)
    added = jnp.zeros((ROWS_OWN, CX), F32)
    for slot in range(0, SLOTS, 2):
        left, right = [], []
        for k in (slot, slot + 1):
            at_l = row_l == layer[k : k + 1]
            at_x = row_x == column[k : k + 1]
            left.append(
                jnp.concatenate(
                    [
                        jnp.where(at_l, sources[k * COMP + c : k * COMP + c + 1, :], 0.0)
                        for c in range(COMP)
                    ],
                    axis=0,
                ).astype(BF16)
            )
            right.append(jnp.where(at_x, 1.0, 0.0).astype(BF16))
        added += dot(jnp.concatenate(left, axis=1), jnp.concatenate(right, axis=1), NT)
    edges = jnp.concatenate([xl[:, :ROWS_OWN], xr[:, :ROWS_OWN]], axis=0)
    place = iota((4, LANES), 0)
    place = jnp.where(place < 2, place - 2, place + CX - 2)
    far = jnp.abs(place - iota((4, LANES), 1))
    stencil = jnp.where(far == 1, 16.0, jnp.where(far == 2, -1.0, 0.0))
    added += dot(edges, stencil, TN, HIGHEST) * (1.0 / 12.0)
    out[...] = partial[...] + HALF_STEP * added.reshape(COMP, CZ, CY, CX)


def call(kernel, outs, scratch=(), smem=(), count=0):
    specs = [
        pl.BlockSpec(memory_space=pltpu.SMEM if k in smem else pltpu.VMEM) for k in range(count)
    ]
    return pl.pallas_call(
        kernel,
        out_shape=outs,
        in_specs=specs,
        scratch_shapes=scratch,
        name=kernel.__name__,
        compiler_params=pltpu.CompilerParams(vmem_limit_bytes=VMEM_GRANT),
    )


def shape(dims, dtype=F32):
    return jax.ShapeDtypeStruct(dims, dtype)


def neighbours(axis):
    count = lax.axis_size(axis)
    forward = [(i, i + 1) for i in range(count - 1)]
    return forward, [(b, a) for a, b in forward]


def shards(
    field_h,
    field_p,
    potential,
    coupling,
    wt_cells,
    wt_coords,
    wt_patch,
    patch_coef,
    sph_points,
    sph_cells,
    sph_frac,
):
    z_count = lax.axis_size("gz")
    core = (lax.axis_index("gy") % 2).reshape(1)
    xy_count = lax.axis_size("gx") * lax.axis_size("gy")
    up, down = neighbours("gz")
    zl = lax.ppermute(field_h[:, CZ - 2 :], "gz", up)
    zh = lax.ppermute(field_h[:, :2], "gz", down)
    slab = shape((ROWS_SLAB, LANES))
    first, last = call(y_slab_kernel, (slab, slab), count=3)(field_h, zl, zh)
    up, down = neighbours("gy")
    yl = lax.ppermute(last, "gy", up)
    yh = lax.ppermute(first, "gy", down)
    grid = (field_h, zl, zh, yl, yh)
    edge = shape((2, ROWS_ALL))
    first, last = call(x_edge_kernel, (edge, edge), count=5)(*grid)
    up, down = neighbours("gx")
    xl = lax.ppermute(last, "gx", up)
    xr = lax.ppermute(first, "gx", down)
    inner = call(interior_points_kernel, shape((COMP, LANES)), count=7)(
        *grid, sph_cells, sph_frac
    )
    cube = shape((COMP, CZ, CY, CX))
    section_h, partial = call(right_side_kernel, (cube, cube), count=8, smem=(7,))(
        *grid, field_p, potential, coupling
    )
    packed = call(
        pack_kernel, shape((z_count, SENT_ROWS, LANES), BF16), count=8, smem=(0,)
    )(
        core,
        inner,
        xl,
        xr,
        sph_cells,
        sph_frac,
        sph_points.reshape(1, LANES),
        patch_coef[0],
    )
    arrived = lax.all_to_all(packed, "gz", 0, 0, tiled=True)
    partner = lax.ppermute(arrived, "gy", [(i, i ^ 1) for i in range(lax.axis_size("gy"))])
    radial, angular = mode_factors()
    sent = call(
        partial_modes_kernel,
        shape((xy_count, MODE_ROWS, LANES), BF16),
        scratch=[pltpu.VMEM((MODE_ROWS, LANES), F32)],
        count=3,
    )(arrived, jnp.asarray(radial), jnp.asarray(angular))
    gathered = lax.all_to_all(sent, ("gx", "gy"), 0, 0, tiled=True)
    section_p = call(
        source_kernel,
        cube,
        scratch=[
            pltpu.VMEM((3, CHEB * SLOTS, LANES), F32),
            pltpu.VMEM((SLOTS * 40, LANES), F32),
            pltpu.VMEM((SLOTS * COMP, LANES), F32),
        ],
        count=9,
        smem=(0, 1),
    )(
        core,
        wt_patch.reshape(SLOTS),
        arrived,
        partner,
        jnp.moveaxis(wt_coords[0, 0, 0], 1, 0),
        wt_cells[0, 0, 0],
        partial,
        xl,
        xr,
    )
    modes = call(sum_modes_kernel, shape((COMP, 1, NMODE)), count=1)(gathered)
    return section_h, section_p, jnp.moveaxis(modes, 1, 0)


def solution(mesh):
    placed = (
        P(None, "gz", "gy", "gx"),
        P(None, "gz", "gy", "gx"),
        P("gz", "gy", "gx"),
        P(),
        P("gz", "gy", "gx", None, None),
        P("gz", "gy", "gx", None, None, None),
        P("gz", "gy", "gx", None, None),
        P("gz", None, None, None),
        P(("gx", "gy", "gz")),
        P(None, ("gx", "gy", "gz")),
        P(None, ("gx", "gy", "gz")),
    )
    return jax.shard_map(
        shards,
        mesh=mesh,
        in_specs=placed,
        out_specs=(P(None, "gz", "gy", "gx"), P(None, "gz", "gy", "gx"), P("gz", None, None)),
        check_vma=False,
    )
```

```python
import functools

import jax
import jax.numpy as jnp
import numpy as np
from jax import lax
from jax.experimental import pallas as pl
from jax.experimental.pallas import tpu as pltpu
from jax.sharding import PartitionSpec as P

LMAX = 30
NTHETA = 32
NPHI = 64
NANG = NTHETA * NPHI
NMODE = (LMAX + 1) ** 2
HALF_STEP = 0.125

COMP = 10
CZ = 4
CY = 8
CX = 128
LANES = 128
ROWS_OWN = COMP * CZ * CY
ROWS_SLAB = COMP * 2 * CY
ROWS_ALL = ROWS_OWN + 4 * ROWS_SLAB
MODE_TILES = 8
MODE_ROWS = COMP * MODE_TILES
CHEB = 8
HALF = COMP // 2
POINT_ROWS = COMP + 2
SENT_ROWS = 32
SLOTS = 8
VMEM_GRANT = 8 << 20

F32 = jnp.float32
BF16 = jnp.bfloat16
HIGHEST = lax.Precision.HIGHEST
NN = (((1,), (0,)), ((), ()))
NT = (((1,), (1,)), ((), ()))
TN = (((0,), (0,)), ((), ()))


def mode_factors():
    polar = np.pi * (np.arange(NTHETA) + 0.5) / NTHETA
    azimuth = 2.0 * np.pi * np.arange(NPHI) / NPHI
    cosine, sine = np.cos(polar), np.sin(polar)
    legendre = np.zeros((LMAX + 1, LMAX + 1, NTHETA))
    diagonal = np.full(NTHETA, np.sqrt(0.25 / np.pi))
    for m in range(LMAX + 1):
        if m > 0:
            diagonal = diagonal * sine * np.sqrt((2.0 * m + 1.0) / (2.0 * m))
        legendre[m, m] = diagonal
        if m < LMAX:
            legendre[m + 1, m] = cosine * np.sqrt(2.0 * m + 3.0) * diagonal
        for l in range(m + 2, LMAX + 1):
            a = np.sqrt((4.0 * l * l - 1.0) / (l * l - m * m))
            b = np.sqrt(((l - 1.0) ** 2 - m * m) / (4.0 * (l - 1.0) ** 2 - 1.0))
            legendre[l, m] = a * (cosine * legendre[l - 1, m] - b * legendre[l - 2, m])
    width = MODE_TILES * LANES
    radial = np.zeros((NTHETA, width))
    angular = np.zeros((NPHI, width))
    weight = sine * np.pi / NTHETA
    for l in range(LMAX + 1):
        for m in range(-l, l + 1):
            n = l * l + l + m
            radial[:, n] = legendre[l, abs(m)] * weight
            if m == 0:
                angular[:, n] = 1.0
            elif m > 0:
                angular[:, n] = np.sqrt(2.0) * np.cos(m * azimuth)
            else:
                angular[:, n] = np.sqrt(2.0) * np.sin(-m * azimuth)
    angular = angular.astype(np.float32)
    high = angular.astype(jnp.bfloat16)
    low = (angular - high.astype(np.float32)).astype(jnp.bfloat16)
    return radial.astype(np.float32), np.concatenate([high, low], axis=0)


def iota(shape, dim):
    return lax.broadcasted_iota(jnp.int32, shape, dim)


def split2(value):
    high = value.astype(BF16)
    return high, (value - high.astype(F32)).astype(BF16)


def dot(a, b, dims, precision=None):
    return lax.dot_general(a, b, dims, precision=precision, preferred_element_type=F32)


def two_hot(position, cell, fraction):
    return jnp.where(position == cell, 1.0 - fraction, 0.0) + jnp.where(
        position == cell + 1, fraction, 0.0
    )


def weighted_rows(parts, plan):
    own, zl, zh, yl, yh = parts
    rows = []
    for c in range(COMP):
        total = jnp.zeros((8, LANES), F32)
        for z in range(CZ):
            base = (c * CZ + z) * CY
            total += own[base : base + 8] * plan[(z + 2) * 8 : (z + 3) * 8]
        for z in range(2):
            base = (c * 2 + z) * CY
            total += zl[base : base + 8] * plan[z * 8 : z * 8 + 8]
            total += zh[base : base + 8] * plan[(z + 6) * 8 : (z + 7) * 8]
            base = c * 16 + z * 8
            total += yl[base : base + 8] * plan[64 + z * 8 : 72 + z * 8]
            total += yh[base : base + 8] * plan[80 + z * 8 : 88 + z * 8]
        rows.append(jnp.sum(total, axis=0, keepdims=True))
    return jnp.concatenate(rows, axis=0)


def prep_kernel(
    core, cells, frac, points, coef, coords, wt_cells, p, v, k, q,
    wide, plan, node, main, rest, high, low, series, target,
):
    cell, fraction = cells[...], frac[...]
    wide_high, wide_low = split2(two_hot(iota((CX, LANES), 0) + 2, cell[2:3], fraction[2:3]))
    wide[0] = wide_high
    wide[1] = wide_low
    row8 = iota((8, LANES), 0)
    row16 = iota((16, LANES), 0)
    wy = two_hot(row8 + 2, cell[1:2], fraction[1:2])
    for z in range(CZ + 4):
        plan[z * 8 : z * 8 + 8, :] = two_hot(z, cell[0:1], fraction[0:1]) * wy
    wz = two_hot(row16 // 2, cell[0:1], fraction[0:1])
    plan[64:80, :] = wz * two_hot(row16 % 2, cell[1:2], fraction[1:2])
    plan[80:96, :] = wz * two_hot(row16 % 2 + CY + 2, cell[1:2], fraction[1:2])
    place = jnp.where(row8 < 2, row8, row8 + CX)
    plan[96:104, :] = two_hot(place, cell[2:3], fraction[2:3])
    point = points[...]
    node[0:1, :] = (point // NANG).astype(F32)
    node[1:2, :] = (point // NPHI % NTHETA).astype(F32)
    node[2:3, :] = (point % NPHI).astype(F32)
    quarter = [
        jnp.concatenate(
            [jnp.where(core[0] % 2 == 0, coef[c, 0:4, :], coef[c, 4:8, :]) for c in (a, a + HALF)],
            axis=1,
        )
        for a in range(HALF)
    ]
    main[...] = jnp.concatenate(quarter[:4], axis=0).astype(BF16)
    rest[...] = quarter[4]
    for axis in range(3):
        value = coords[axis]
        older, newer = jnp.ones_like(value), value
        for n in range(CHEB):
            series[axis, n * SLOTS : (n + 1) * SLOTS, :] = older
            older, newer = newer, 2.0 * value * newer - older
    for slot in range(SLOTS):
        third = series[2, pl.ds(slot, CHEB, stride=SLOTS), :]
        product = jnp.concatenate(
            [series[1, n * SLOTS + slot : n * SLOTS + slot + 1, :] * third for n in range(CHEB)],
            axis=0,
        )
        high[slot], low[slot] = split2(product)
    cell = wt_cells[...]
    target[0] = (cell // CX).astype(F32)
    target[1] = (cell % CX).astype(F32)


def edges_kernel(height, spot, h, zl, zh, base, plan, first, last, far, lower, upper):
    low, high = zl[...].astype(F32), zh[...].astype(F32)
    for c in range(COMP):
        for z in range(CZ + 4):
            if z < 2:
                source = low[(c * 2 + z) * CY : (c * 2 + z + 1) * CY]
            elif z < CZ + 2:
                source = h[c, z - 2]
            else:
                source = high[(c * 2 + z - 6) * CY : (c * 2 + z - 5) * CY]
            row = (c * (CZ + 4) + z) * 2
            lower[row : row + 2, :] = source[0:2]
            upper[row : row + 2, :] = source[CY - 2 : CY]
    below, above = lower[...].astype(BF16), upper[...].astype(BF16)
    first[...] = below
    last[...] = above
    row = iota((8, LANES), 0)
    lane = iota((8, LANES), 1)
    place = jnp.where(row < 2, row, row + CX - 4)
    pick = jnp.where(lane == place, 1.0, 0.0).astype(BF16)
    own = h[...].reshape(ROWS_OWN, LANES).astype(BF16)
    wide = jnp.concatenate([dot(pick, part, NT) for part in (own, zl[...], zh[...])], axis=1)
    empty = jnp.zeros((8, 2 * LANES - ROWS_SLAB), F32)

    def block(edge, start):
        tiles = edge.shape[1] // LANES
        rows = [
            edge[j : j + 1, t * LANES : (t + 1) * LANES]
            for j in (start, start + 1)
            for t in range(tiles)
        ]
        rows.append(jnp.zeros((16 - len(rows), LANES), F32))
        return jnp.concatenate(rows, axis=0).astype(BF16)

    below = jnp.concatenate([dot(pick, below, NT), empty], axis=1)
    above = jnp.concatenate([dot(pick, above, NT), empty], axis=1)
    blocks = [[block(edge, start) for start in (0, 2)] for edge in (wide, below, above)]
    column, level = spot[0] // height, spot[0] % height
    for e in range(far.shape[0]):
        right = e // height == column + 1
        inner, lower_row, upper_row = [jnp.where(right, hi, lo) for lo, hi in blocks]
        outer = jnp.where(e % height == level + 1, upper_row, lower_row)
        far[e] = jnp.where(e % height == level, inner, outer)


def middle_kernel(h, zl, zh, yl, yh, wide, plan, base, out, partial):
    high, low = split2(h[...].reshape(ROWS_OWN, LANES))
    near, fine = wide[0], wide[1]
    parts = [dot(high, near, NN) + dot(low, near, NN) + dot(high, fine, NN)]
    parts += [dot(slab[...], near, NN) + dot(slab[...], fine, NN) for slab in (zl, zh, yl, yh)]
    out[...] = weighted_rows(parts, plan[...])
    z_low, z_high = zl[...].astype(F32), zh[...].astype(F32)
    y_low, y_high = yl[...].astype(F32), yh[...].astype(F32)
    gap = jnp.zeros((CY - 4, LANES), F32)
    for c in range(COMP):
        at = c * 2 * CY
        two_back, one_back = z_low[at : at + CY], z_low[at + CY : at + 2 * CY]
        one_on, two_on = z_high[at : at + CY], z_high[at + CY : at + 2 * CY]
        along_z = [16.0 * one_back - two_back, -one_back, -one_on, 16.0 * one_on - two_on]
        for z in range(CZ):
            at = (c * (CZ + 4) + z + 2) * 2
            below, above = y_low[at : at + 2], y_high[at : at + 2]
            along_y = jnp.concatenate(
                [
                    16.0 * below[1:2] - below[0:1],
                    -below[1:2],
                    gap,
                    -above[0:1],
                    16.0 * above[0:1] - above[1:2],
                ],
                axis=0,
            )
            partial[c, z] = base[c, z] + (HALF_STEP / 12.0) * (along_z[z] + along_y)


def pack_kernel(height, spot, inner, far, plan, node, main, rest, out, near):
    column, level = spot[0] // height, spot[0] % height
    width = far.shape[0] // height

    def edge(rise, lanes):
        tiles = -(-lanes // LANES)
        rows = []
        for side in (-1, 1):
            at, up = column + side, level + rise
            inside = (at >= 0) & (at < width) & (up >= 0) & (up < height)
            source = jnp.clip(at, 0, width - 1) * height + jnp.clip(up, 0, height - 1)
            block = jnp.where(inside, far[source].astype(F32), 0.0)
            for j in range(2):
                pieces = [block[j * tiles + t : j * tiles + t + 1] for t in range(tiles)]
                rows.append(jnp.concatenate(pieces, axis=1)[:, :lanes])
        return jnp.concatenate(rows, axis=0)

    beside = edge(0, ROWS_OWN + 2 * ROWS_SLAB)
    near[...] = beside[:, :ROWS_OWN]
    edges = jnp.concatenate([beside, edge(-1, ROWS_SLAB), edge(1, ROWS_SLAB)], axis=1)
    grown = dot(edges, plan[96:100, :], TN, HIGHEST)
    cuts = (0, 320, 480, 640, 800, 960)
    parts = [grown[a:b] for a, b in zip(cuts[:-1], cuts[1:])]
    values = inner[...] + weighted_rows(parts, plan[...])
    tail = jnp.concatenate([node[2:3, :], rest[...]], axis=0)
    sphere, polar = node[0:1, :], node[1:2, :]
    coefficients = main[...]
    for s in range(out.shape[0]):
        here = jnp.where(sphere == float(s), polar, 255.0)
        block = jnp.concatenate([values, here, tail], axis=0)
        out[s, 0:16, :] = block.astype(BF16)
        out[s, 16:32, :] = coefficients


def partial_modes_kernel(arrived, radial, angular, out, rows):
    row_i = iota((NTHETA, LANES), 0).astype(F32)
    row_j = iota((NPHI, LANES), 0).astype(F32)
    dense = jnp.zeros((COMP * NTHETA, NPHI), F32)
    for s in range(0, arrived.shape[0], 2):
        left, right = [], []
        for k in (s, s + 1):
            block = arrived[k, 0:16, :].astype(F32)
            at_i = row_i == block[COMP : COMP + 1]
            at_j = row_j == block[COMP + 1 : COMP + 2]
            right.append(jnp.where(at_j, 1.0, 0.0).astype(BF16))
            left.append(
                jnp.concatenate(
                    [jnp.where(at_i, block[c : c + 1], 0.0) for c in range(COMP)], axis=0
                ).astype(BF16)
            )
        dense += dot(jnp.concatenate(left, axis=1), jnp.concatenate(right, axis=1), NT)
    exact = dense.astype(BF16)
    exact = jnp.concatenate([exact, exact], axis=1)
    for t in range(MODE_TILES):
        lanes = slice(t * LANES, (t + 1) * LANES)
        grown = dot(exact, angular[:, lanes], NN)
        weight = radial[:, lanes]
        for c in range(COMP):
            part = grown[c * NTHETA : (c + 1) * NTHETA] * weight
            rows[t * COMP + c : t * COMP + c + 1, :] = jnp.sum(part, axis=0, keepdims=True)
    sent = rows[...].astype(BF16)
    for k in range(out.shape[0]):
        out[k] = sent


def sum_modes_kernel(arrived, out):
    total = arrived[0].astype(F32)
    for k in range(1, arrived.shape[0]):
        total += arrived[k].astype(F32)
    for t in range(MODE_TILES):
        width = min(LANES, NMODE - t * LANES)
        for c in range(COMP):
            row = t * COMP + c
            out[c, :, t * LANES : t * LANES + width] = total[row : row + 1, :width]


def base_kernel(h, p, potential, coupling, section_h, out, staged, sems):
    row = iota((CY, LANES), 0)
    lane = iota((CY, LANES), 1)
    copies = []
    for c in range(COMP):
        for z in range(CZ):
            mid = h[c, z]
            staged[c, z] = mid + HALF_STEP * p[c, z]
        copy = pltpu.make_async_copy(staged.at[c], section_h.at[c], sems.at[c])
        copy.start()
        copies.append(copy)
    for c in range(COMP):
        for z in range(CZ):
            mid = h[c, z]
            total = -90.0 * mid
            for step, factor in ((1, 16.0), (2, -1.0)):
                for at in (z - step, z + step):
                    if 0 <= at < CZ:
                        total += factor * h[c, at]
                up = jnp.where(row < CY - step, pltpu.roll(mid, CY - step, 0), 0.0)
                down = jnp.where(row >= step, pltpu.roll(mid, step, 0), 0.0)
                right = jnp.where(lane < CX - step, pltpu.roll(mid, CX - step, 1), 0.0)
                left = jnp.where(lane >= step, pltpu.roll(mid, step, 1), 0.0)
                total += factor * ((up + down) + (right + left))
            coupled = coupling[c, 0] * h[0, z]
            for b in range(1, COMP):
                coupled += coupling[c, b] * h[b, z]
            out[c, z] = p[c, z] + HALF_STEP * (total * (1.0 / 12.0) - potential[z] * coupled)
    for copy in copies:
        copy.wait()


def source_kernel(
    core, patch, mine, other, high, low, series, target, partial, near_x, out, terms, sources,
    staged, sems,
):
    empty = jnp.zeros((CHEB * CHEB, LANES), BF16)
    for slot in range(SLOTS):
        chosen = patch[slot]
        first, second = mine[chosen], other[chosen]
        block = jnp.concatenate([first[16:32], second[16:32], first[0:16], second[0:16]], axis=0)
        grown = jnp.zeros((64, 2 * LANES), F32)
        for part in (high[slot], low[slot]):
            wide = jnp.concatenate(
                [jnp.concatenate([part, empty], axis=0), jnp.concatenate([empty, part], axis=0)],
                axis=1,
            )
            grown += dot(block, wide, NN)
        start = series[0, pl.ds(slot, 4, stride=SLOTS), :]
        end = series[0, pl.ds(slot + 4 * SLOTS, 4, stride=SLOTS), :]
        near = jnp.where(core[0] % 2 == 0, start, end)
        far = jnp.where(core[0] % 2 == 0, end, start)
        near, far = jnp.concatenate([near] * 4, axis=0), jnp.concatenate([far] * 4, axis=0)
        for side in range(2):
            lanes = slice(side * LANES, (side + 1) * LANES)
            main = grown[0:16, lanes] * near + grown[16:32, lanes] * far
            rest = grown[44:48, lanes] * near[0:4] + grown[60:64, lanes] * far[0:4]
            row = (slot * 2 + side) * 20
            terms[row : row + 16, :] = main
            terms[row + 16 : row + 20, :] = rest
    count = SLOTS * COMP
    total = terms[pl.ds(0, count, stride=4), :]
    for m in range(1, 4):
        total += terms[pl.ds(m, count, stride=4), :]
    sources[...] = total
    row_l = iota((CZ * CY, LANES), 0).astype(F32)
    row_x = iota((CX, LANES), 0).astype(F32)
    added = jnp.zeros((ROWS_OWN, CX), F32)
    for slot in range(0, SLOTS, 2):
        left, right = [], []
        for k in (slot, slot + 1):
            at_l = jnp.where(row_l == target[0, k : k + 1, :], 1.0, 0.0).astype(BF16)
            at_x = jnp.where(row_x == target[1, k : k + 1, :], 1.0, 0.0).astype(BF16)
            pieces = []
            for c in range(COMP):
                row = k * COMP + c
                value = jnp.broadcast_to(sources[row : row + 1, :], (16, LANES)).astype(BF16)
                pieces += [at_l[0:16] * value, at_l[16:32] * value]
            left.append(jnp.concatenate(pieces, axis=0))
            right.append(at_x)
        added += dot(jnp.concatenate(left, axis=1), jnp.concatenate(right, axis=1), NT)
    place = iota((4, LANES), 0)
    place = jnp.where(place < 2, place - 2, place + CX - 2)
    gap = jnp.abs(place - iota((4, LANES), 1))
    stencil = jnp.where(gap == 1, 16.0, jnp.where(gap == 2, -1.0, 0.0))
    added += dot(near_x[...], stencil, TN, HIGHEST) * (1.0 / 12.0)
    added = added.reshape(COMP, CZ, CY, CX)
    copies = []
    for c in range(COMP):
        staged[c] = partial[c] + HALF_STEP * added[c]
        copy = pltpu.make_async_copy(staged.at[c], out.at[c], sems.at[c])
        copy.start()
        copies.append(copy)
    for copy in copies:
        copy.wait()


def call(kernel, outs, scratch=(), smem=(), count=0, whole=(), kept=()):
    def spec(k, small=(), large=()):
        space = pltpu.SMEM if k in small else pl.ANY if k in large else pltpu.VMEM
        return pl.BlockSpec(memory_space=space)

    single = not isinstance(outs, tuple)
    results = (outs,) if single else outs
    out_specs = tuple(spec(k, large=kept) for k in range(len(results)))
    return pl.pallas_call(
        kernel,
        out_shape=outs,
        in_specs=[spec(k, smem, whole) for k in range(count)],
        out_specs=out_specs[0] if single else out_specs,
        scratch_shapes=scratch,
        name=getattr(kernel, "func", kernel).__name__,
        compiler_params=pltpu.CompilerParams(vmem_limit_bytes=VMEM_GRANT),
    )


def shape(dims, dtype=F32):
    return jax.ShapeDtypeStruct(dims, dtype)


def neighbours(axis):
    count = lax.axis_size(axis)
    forward = [(i, i + 1) for i in range(count - 1)]
    return forward, [(b, a) for a, b in forward]


def shards(
    field_h,
    field_p,
    potential,
    coupling,
    wt_cells,
    wt_coords,
    wt_patch,
    patch_coef,
    sph_points,
    sph_cells,
    sph_frac,
):
    z_count = lax.axis_size("gz")
    height = lax.axis_size("gy")
    patch = wt_patch.reshape(SLOTS)
    core = lax.axis_index(("gx", "gy")).reshape(1)
    xy_count = lax.axis_size("gx") * lax.axis_size("gy")
    up, down = neighbours("gz")
    top = field_h[:, CZ - 2 :].astype(BF16).reshape(ROWS_SLAB, LANES)
    bottom = field_h[:, :2].astype(BF16).reshape(ROWS_SLAB, LANES)
    zl = lax.ppermute(top, "gz", up)
    zh = lax.ppermute(bottom, "gz", down)
    wide, plan, node, main, rest, high, low, series, target = call(
        prep_kernel,
        (
            shape((2, CX, LANES), BF16),
            shape((104, LANES)),
            shape((3, LANES)),
            shape((16, LANES), BF16),
            shape((4, LANES)),
            shape((SLOTS, CHEB * CHEB, LANES), BF16),
            shape((SLOTS, CHEB * CHEB, LANES), BF16),
            shape((3, CHEB * SLOTS, LANES)),
            shape((2, SLOTS, LANES)),
        ),
        count=11,
        smem=(0,),
    )(
        core,
        sph_cells,
        sph_frac,
        sph_points.reshape(1, LANES),
        patch_coef[0],
        jnp.moveaxis(wt_coords[0, 0, 0], 1, 0),
        wt_cells[0, 0, 0],
        field_p,
        potential,
        coupling,
        patch,
    )
    slab = shape((ROWS_SLAB, LANES), BF16)
    pad = pltpu.VMEM((ROWS_SLAB, LANES), F32)
    cube = shape((COMP, CZ, CY, CX))
    stage = [pltpu.VMEM((COMP, CZ, CY, CX), F32), pltpu.SemaphoreType.DMA((COMP,))]
    section_h, base = call(
        base_kernel, (cube, cube), scratch=stage, count=4, smem=(3,), kept=(0,)
    )(field_h, field_p, potential, coupling)
    first, last, far = call(
        functools.partial(edges_kernel, height),
        (slab, slab, shape((xy_count, 16, LANES), BF16)),
        scratch=[pad, pad],
        count=6,
        smem=(0,),
        whole=(4, 5),
    )(core, field_h, zl, zh, base, plan)
    far = lax.all_to_all(far, ("gx", "gy"), 0, 0, tiled=True)
    up, down = neighbours("gy")
    yl = lax.ppermute(last, "gy", up)
    yh = lax.ppermute(first, "gy", down)
    grid = (field_h, zl, zh, yl, yh)
    inner, partial = call(middle_kernel, (shape((COMP, LANES)), cube), count=8)(
        *grid, wide, plan, base
    )
    packed, near_x = call(
        functools.partial(pack_kernel, height),
        (shape((z_count, SENT_ROWS, LANES), BF16), shape((4, ROWS_OWN))),
        count=7,
        smem=(0,),
    )(core, inner, far, plan, node, main, rest)
    arrived = lax.all_to_all(packed, "gz", 0, 0, tiled=True)
    partner = lax.ppermute(arrived, "gy", [(i, i ^ 1) for i in range(lax.axis_size("gy"))])
    radial, angular = mode_factors()
    sent = call(
        partial_modes_kernel,
        shape((xy_count, MODE_ROWS, LANES), BF16),
        scratch=[
            pltpu.VMEM((MODE_ROWS, LANES), F32),
        ],
        count=3,
    )(arrived, jnp.asarray(radial), jnp.asarray(angular))
    gathered = lax.all_to_all(sent, ("gx", "gy"), 0, 0, tiled=True)
    section_p = call(
        source_kernel,
        cube,
        scratch=[
            pltpu.VMEM((SLOTS * 40, LANES), F32),
            pltpu.VMEM((SLOTS * COMP, LANES), F32),
            *stage,
        ],
        count=10,
        smem=(0, 1),
        kept=(0,),
    )(
        core,
        patch,
        arrived,
        partner,
        high,
        low,
        series,
        target,
        partial,
        near_x,
    )
    modes = call(sum_modes_kernel, shape((COMP, 1, NMODE)), count=1)(gathered)
    return section_h, section_p, jnp.moveaxis(modes, 1, 0)


def solution(mesh):
    placed = (
        P(None, "gz", "gy", "gx"),
        P(None, "gz", "gy", "gx"),
        P("gz", "gy", "gx"),
        P(),
        P("gz", "gy", "gx", None, None),
        P("gz", "gy", "gx", None, None, None),
        P("gz", "gy", "gx", None, None),
        P("gz", None, None, None),
        P(("gx", "gy", "gz")),
        P(None, ("gx", "gy", "gz")),
        P(None, ("gx", "gy", "gz")),
    )
    return jax.shard_map(
        shards,
        mesh=mesh,
        in_specs=placed,
        out_specs=(P(None, "gz", "gy", "gx"), P(None, "gz", "gy", "gx"), P("gz", None, None)),
        check_vma=False,
    )
```

```python
import functools

import jax
import jax.numpy as jnp
import numpy as np
from jax import lax
from jax.experimental import pallas as pl
from jax.experimental.pallas import tpu as pltpu
from jax.sharding import PartitionSpec as P

LMAX = 30
NTHETA = 32
NPHI = 64
NANG = NTHETA * NPHI
NMODE = (LMAX + 1) ** 2
HALF_STEP = 0.125

COMP = 10
CZ = 4
CY = 8
CX = 128
LANES = 128
ROWS_OWN = COMP * CZ * CY
ROWS_SLAB = COMP * 2 * CY
ROWS_ALL = ROWS_OWN + 4 * ROWS_SLAB
MODE_TILES = 8
MODE_ROWS = COMP * MODE_TILES
CHEB = 8
HALF = COMP // 2
POINT_ROWS = COMP + 2
SENT_ROWS = 32
SLOTS = 8
VMEM_GRANT = 8 << 20
PLANE = 64

F32 = jnp.float32
BF16 = jnp.bfloat16
HIGHEST = lax.Precision.HIGHEST
NN = (((1,), (0,)), ((), ()))
NT = (((1,), (1,)), ((), ()))
TN = (((0,), (0,)), ((), ()))


def mode_factors():
    polar = np.pi * (np.arange(NTHETA) + 0.5) / NTHETA
    azimuth = 2.0 * np.pi * np.arange(NPHI) / NPHI
    cosine, sine = np.cos(polar), np.sin(polar)
    legendre = np.zeros((LMAX + 1, LMAX + 1, NTHETA))
    diagonal = np.full(NTHETA, np.sqrt(0.25 / np.pi))
    for m in range(LMAX + 1):
        if m > 0:
            diagonal = diagonal * sine * np.sqrt((2.0 * m + 1.0) / (2.0 * m))
        legendre[m, m] = diagonal
        if m < LMAX:
            legendre[m + 1, m] = cosine * np.sqrt(2.0 * m + 3.0) * diagonal
        for l in range(m + 2, LMAX + 1):
            a = np.sqrt((4.0 * l * l - 1.0) / (l * l - m * m))
            b = np.sqrt(((l - 1.0) ** 2 - m * m) / (4.0 * (l - 1.0) ** 2 - 1.0))
            legendre[l, m] = a * (cosine * legendre[l - 1, m] - b * legendre[l - 2, m])
    width = MODE_TILES * LANES
    radial = np.zeros((NTHETA, width))
    angular = np.zeros((NPHI, width))
    weight = sine * np.pi / NTHETA
    for l in range(LMAX + 1):
        for m in range(-l, l + 1):
            n = l * l + l + m
            radial[:, n] = legendre[l, abs(m)] * weight
            if m == 0:
                angular[:, n] = 1.0
            elif m > 0:
                angular[:, n] = np.sqrt(2.0) * np.cos(m * azimuth)
            else:
                angular[:, n] = np.sqrt(2.0) * np.sin(-m * azimuth)
    angular = angular.astype(np.float32)
    high = angular.astype(jnp.bfloat16)
    low = (angular - high.astype(np.float32)).astype(jnp.bfloat16)
    return radial.astype(np.float32), np.concatenate([high, low], axis=0)


def iota(shape, dim):
    return lax.broadcasted_iota(jnp.int32, shape, dim)


def split2(value):
    high = value.astype(BF16)
    return high, (value - high.astype(F32)).astype(BF16)


def dot(a, b, dims, precision=None):
    return lax.dot_general(a, b, dims, precision=precision, preferred_element_type=F32)


def two_hot(position, cell, fraction):
    return jnp.where(position == cell, 1.0 - fraction, 0.0) + jnp.where(
        position == cell + 1, fraction, 0.0
    )


def weighted_rows(parts, plan):
    own, zl, zh, yl, yh = parts
    rows = []
    for c in range(COMP):
        total = jnp.zeros((8, LANES), F32)
        for z in range(CZ):
            base = (c * CZ + z) * CY
            total += own[base : base + 8] * plan[(z + 2) * 8 : (z + 3) * 8]
        for z in range(2):
            base = (c * 2 + z) * CY
            total += zl[base : base + 8] * plan[z * 8 : z * 8 + 8]
            total += zh[base : base + 8] * plan[(z + 6) * 8 : (z + 7) * 8]
            base = c * 16 + z * 8
            total += yl[base : base + 8] * plan[64 + z * 8 : 72 + z * 8]
            total += yh[base : base + 8] * plan[80 + z * 8 : 88 + z * 8]
        rows.append(jnp.sum(total, axis=0, keepdims=True))
    return jnp.concatenate(rows, axis=0)


def low_high(even, first, second):
    return jnp.where(even, second, first), jnp.where(even, first, second)


def prep_kernel(
    core, cells, frac, points, coef, coords, wt_cells, p, v, k, q,
    wide, plan, node, main, rest, high, low, series, target,
):
    cell, fraction = cells[...], frac[...]
    wide_high, wide_low = split2(two_hot(iota((CX, LANES), 0) + 2, cell[2:3], fraction[2:3]))
    wide[0] = wide_high
    wide[1] = wide_low
    row8 = iota((8, LANES), 0)
    row16 = iota((16, LANES), 0)
    wy = two_hot(row8 + 2, cell[1:2], fraction[1:2])
    for z in range(CZ + 4):
        plan[z * 8 : z * 8 + 8, :] = two_hot(z, cell[0:1], fraction[0:1]) * wy
    wz = two_hot(row16 // 2, cell[0:1], fraction[0:1])
    plan[64:80, :] = wz * two_hot(row16 % 2, cell[1:2], fraction[1:2])
    plan[80:96, :] = wz * two_hot(row16 % 2 + CY + 2, cell[1:2], fraction[1:2])
    place = jnp.where(row8 < 2, row8, row8 + CX)
    plan[96:104, :] = two_hot(place, cell[2:3], fraction[2:3])
    point = points[...]
    node[0:1, :] = (point // NANG).astype(F32)
    node[1:2, :] = (point // NPHI % NTHETA).astype(F32)
    node[2:3, :] = (point % NPHI).astype(F32)
    quarter = [
        jnp.concatenate(
            [jnp.where(core[0] % 2 == 0, coef[c, 0:4, :], coef[c, 4:8, :]) for c in (a, a + HALF)],
            axis=1,
        )
        for a in range(HALF)
    ]
    main[...] = jnp.concatenate(quarter[:4], axis=0).astype(BF16)
    rest[...] = quarter[4]
    for axis in range(3):
        value = coords[axis]
        older, newer = jnp.ones_like(value), value
        for n in range(CHEB):
            series[axis, n * SLOTS : (n + 1) * SLOTS, :] = older
            older, newer = newer, 2.0 * value * newer - older
    for slot in range(SLOTS):
        third = series[2, pl.ds(slot, CHEB, stride=SLOTS), :]
        product = jnp.concatenate(
            [series[1, n * SLOTS + slot : n * SLOTS + slot + 1, :] * third for n in range(CHEB)],
            axis=0,
        )
        high[slot], low[slot] = split2(product)
    cell = wt_cells[...]
    target[0] = (cell // CX).astype(F32)
    target[1] = (cell % CX).astype(F32)


def edges_kernel(height, spot, h, za, zb, base, plan, first, last, far, lower, upper):
    zl, zh = za[...], zb[...]
    low, high = zl.astype(F32), zh.astype(F32)
    for c in range(COMP):
        for z in range(CZ + 4):
            if z < 2:
                source = low[(c * 2 + z) * CY : (c * 2 + z + 1) * CY]
            elif z < CZ + 2:
                source = h[c, z - 2]
            else:
                source = high[(c * 2 + z - 6) * CY : (c * 2 + z - 5) * CY]
            row = (c * (CZ + 4) + z) * 2
            lower[row : row + 2, :] = source[0:2]
            upper[row : row + 2, :] = source[CY - 2 : CY]
    below, above = lower[...].astype(BF16), upper[...].astype(BF16)
    last[...], first[...] = low_high(spot[0] % 2 == 0, above, below)
    row = iota((8, LANES), 0)
    lane = iota((8, LANES), 1)
    place = jnp.where(row < 2, row, row + CX - 4)
    pick = jnp.where(lane == place, 1.0, 0.0).astype(BF16)
    own = h[...].reshape(ROWS_OWN, LANES).astype(BF16)
    wide = jnp.concatenate([dot(pick, part, NT) for part in (own, zl, zh)], axis=1)
    empty = jnp.zeros((8, 2 * LANES - ROWS_SLAB), F32)

    def block(edge, start):
        tiles = edge.shape[1] // LANES
        rows = [
            edge[j : j + 1, t * LANES : (t + 1) * LANES]
            for j in (start, start + 1)
            for t in range(tiles)
        ]
        rows.append(jnp.zeros((16 - len(rows), LANES), F32))
        return jnp.concatenate(rows, axis=0).astype(BF16)

    below = jnp.concatenate([dot(pick, below, NT), empty], axis=1)
    above = jnp.concatenate([dot(pick, above, NT), empty], axis=1)
    blocks = [[block(edge, start) for start in (0, 2)] for edge in (wide, below, above)]
    column, level = spot[0] % PLANE // height, spot[0] % height
    for e in range(far.shape[0]):
        right = e // height == column + 1
        inner, lower_row, upper_row = [jnp.where(right, hi, lo) for lo, hi in blocks]
        outer = jnp.where(e % height == level + 1, upper_row, lower_row)
        far[e] = jnp.where(e % height == level, inner, outer)


def middle_kernel(spot, h, za, zb, ya, yb, wide, plan, base, out, partial):
    zl, zh = za[...], zb[...]
    yl, yh = low_high(spot[0] % 2 == 0, ya[...], yb[...])
    high, low = split2(h[...].reshape(ROWS_OWN, LANES))
    near, fine = wide[0], wide[1]
    parts = [dot(high, near, NN) + dot(low, near, NN) + dot(high, fine, NN)]
    parts += [dot(slab, near, NN) + dot(slab, fine, NN) for slab in (zl, zh, yl, yh)]
    out[...] = weighted_rows(parts, plan[...])
    z_low, z_high = zl.astype(F32), zh.astype(F32)
    y_low, y_high = yl.astype(F32), yh.astype(F32)
    gap = jnp.zeros((CY - 4, LANES), F32)
    for c in range(COMP):
        at = c * 2 * CY
        two_back, one_back = z_low[at : at + CY], z_low[at + CY : at + 2 * CY]
        one_on, two_on = z_high[at : at + CY], z_high[at + CY : at + 2 * CY]
        along_z = [16.0 * one_back - two_back, -one_back, -one_on, 16.0 * one_on - two_on]
        for z in range(CZ):
            at = (c * (CZ + 4) + z + 2) * 2
            below, above = y_low[at : at + 2], y_high[at : at + 2]
            along_y = jnp.concatenate(
                [
                    16.0 * below[1:2] - below[0:1],
                    -below[1:2],
                    gap,
                    -above[0:1],
                    16.0 * above[0:1] - above[1:2],
                ],
                axis=0,
            )
            partial[c, z] = base[c, z] + (HALF_STEP / 12.0) * (along_z[z] + along_y)


def pack_kernel(height, spot, inner, far, plan, node, main, rest, out, near):
    column, level = spot[0] % PLANE // height, spot[0] % height
    width = far.shape[0] // height

    def edge(rise, lanes):
        tiles = -(-lanes // LANES)
        rows = []
        for side in (-1, 1):
            at, up = column + side, level + rise
            inside = (at >= 0) & (at < width) & (up >= 0) & (up < height)
            source = jnp.clip(at, 0, width - 1) * height + jnp.clip(up, 0, height - 1)
            block = jnp.where(inside, far[source].astype(F32), 0.0)
            for j in range(2):
                pieces = [block[j * tiles + t : j * tiles + t + 1] for t in range(tiles)]
                rows.append(jnp.concatenate(pieces, axis=1)[:, :lanes])
        return jnp.concatenate(rows, axis=0)

    beside = edge(0, ROWS_OWN + 2 * ROWS_SLAB)
    near[...] = beside[:, :ROWS_OWN]
    edges = jnp.concatenate([beside, edge(-1, ROWS_SLAB), edge(1, ROWS_SLAB)], axis=1)
    grown = dot(edges, plan[96:100, :], TN, HIGHEST)
    cuts = (0, 320, 480, 640, 800, 960)
    parts = [grown[a:b] for a, b in zip(cuts[:-1], cuts[1:])]
    values = inner[...] + weighted_rows(parts, plan[...])
    tail = jnp.concatenate([node[2:3, :], rest[...]], axis=0)
    sphere, polar = node[0:1, :], node[1:2, :]
    coefficients = main[...]
    for s in range(out.shape[0]):
        here = jnp.where(sphere == float(s), polar, 255.0)
        block = jnp.concatenate([values, here, tail], axis=0)
        out[s, 0:16, :] = block.astype(BF16)
        out[s, 16:32, :] = coefficients


def partial_modes_kernel(arrived, radial, angular, out, rows):
    row_i = iota((NTHETA, LANES), 0).astype(F32)
    row_j = iota((NPHI, LANES), 0).astype(F32)
    dense = jnp.zeros((COMP * NTHETA, NPHI), F32)
    for s in range(0, arrived.shape[0], 2):
        left, right = [], []
        for k in (s, s + 1):
            block = arrived[k, 0:16, :].astype(F32)
            at_i = row_i == block[COMP : COMP + 1]
            at_j = row_j == block[COMP + 1 : COMP + 2]
            right.append(jnp.where(at_j, 1.0, 0.0).astype(BF16))
            left.append(
                jnp.concatenate(
                    [jnp.where(at_i, block[c : c + 1], 0.0) for c in range(COMP)], axis=0
                ).astype(BF16)
            )
        dense += dot(jnp.concatenate(left, axis=1), jnp.concatenate(right, axis=1), NT)
    exact = dense.astype(BF16)
    exact = jnp.concatenate([exact, exact], axis=1)
    for t in range(MODE_TILES):
        lanes = slice(t * LANES, (t + 1) * LANES)
        grown = dot(exact, angular[:, lanes], NN)
        weight = radial[:, lanes]
        for c in range(COMP):
            part = grown[c * NTHETA : (c + 1) * NTHETA] * weight
            rows[t * COMP + c : t * COMP + c + 1, :] = jnp.sum(part, axis=0, keepdims=True)
    sent = rows[...].astype(BF16)
    for k in range(out.shape[0]):
        out[k] = sent


def sum_modes_kernel(arrived, out):
    total = arrived[0].astype(F32)
    for k in range(1, arrived.shape[0]):
        total += arrived[k].astype(F32)
    for t in range(MODE_TILES):
        width = min(LANES, NMODE - t * LANES)
        for c in range(COMP):
            row = t * COMP + c
            out[c, :, t * LANES : t * LANES + width] = total[row : row + 1, :width]


def base_kernel(h, p, potential, coupling, section_h, out, staged, sems):
    row = iota((CY, LANES), 0)
    lane = iota((CY, LANES), 1)
    copies = []
    for c in range(COMP):
        for z in range(CZ):
            mid = h[c, z]
            staged[c, z] = mid + HALF_STEP * p[c, z]
        copy = pltpu.make_async_copy(staged.at[c], section_h.at[c], sems.at[c])
        copy.start()
        copies.append(copy)
    for c in range(COMP):
        for z in range(CZ):
            mid = h[c, z]
            total = -90.0 * mid
            for step, factor in ((1, 16.0), (2, -1.0)):
                for at in (z - step, z + step):
                    if 0 <= at < CZ:
                        total += factor * h[c, at]
                up = jnp.where(row < CY - step, pltpu.roll(mid, CY - step, 0), 0.0)
                down = jnp.where(row >= step, pltpu.roll(mid, step, 0), 0.0)
                right = jnp.where(lane < CX - step, pltpu.roll(mid, CX - step, 1), 0.0)
                left = jnp.where(lane >= step, pltpu.roll(mid, step, 1), 0.0)
                total += factor * ((up + down) + (right + left))
            coupled = coupling[c, 0] * h[0, z]
            for b in range(1, COMP):
                coupled += coupling[c, b] * h[b, z]
            out[c, z] = p[c, z] + HALF_STEP * (total * (1.0 / 12.0) - potential[z] * coupled)
    for copy in copies:
        copy.wait()


def source_kernel(
    core, patch, mine, other, high, low, series, target, partial, near_x, out, terms, sources,
    staged, sems,
):
    empty = jnp.zeros((CHEB * CHEB, LANES), BF16)
    for slot in range(SLOTS):
        chosen = patch[slot]
        first, second = mine[chosen], other[chosen]
        block = jnp.concatenate([first[16:32], second[16:32], first[0:16], second[0:16]], axis=0)
        grown = jnp.zeros((64, 2 * LANES), F32)
        for part in (high[slot], low[slot]):
            wide = jnp.concatenate(
                [jnp.concatenate([part, empty], axis=0), jnp.concatenate([empty, part], axis=0)],
                axis=1,
            )
            grown += dot(block, wide, NN)
        start = series[0, pl.ds(slot, 4, stride=SLOTS), :]
        end = series[0, pl.ds(slot + 4 * SLOTS, 4, stride=SLOTS), :]
        near = jnp.where(core[0] % 2 == 0, start, end)
        far = jnp.where(core[0] % 2 == 0, end, start)
        near, far = jnp.concatenate([near] * 4, axis=0), jnp.concatenate([far] * 4, axis=0)
        for side in range(2):
            lanes = slice(side * LANES, (side + 1) * LANES)
            main = grown[0:16, lanes] * near + grown[16:32, lanes] * far
            rest = grown[44:48, lanes] * near[0:4] + grown[60:64, lanes] * far[0:4]
            row = (slot * 2 + side) * 20
            terms[row : row + 16, :] = main
            terms[row + 16 : row + 20, :] = rest
    count = SLOTS * COMP
    total = terms[pl.ds(0, count, stride=4), :]
    for m in range(1, 4):
        total += terms[pl.ds(m, count, stride=4), :]
    sources[...] = total
    row_l = iota((CZ * CY, LANES), 0).astype(F32)
    row_x = iota((CX, LANES), 0).astype(F32)
    added = jnp.zeros((ROWS_OWN, CX), F32)
    for slot in range(0, SLOTS, 2):
        left, right = [], []
        for k in (slot, slot + 1):
            at_l = jnp.where(row_l == target[0, k : k + 1, :], 1.0, 0.0).astype(BF16)
            at_x = jnp.where(row_x == target[1, k : k + 1, :], 1.0, 0.0).astype(BF16)
            pieces = []
            for c in range(COMP):
                row = k * COMP + c
                value = jnp.broadcast_to(sources[row : row + 1, :], (16, LANES)).astype(BF16)
                pieces += [at_l[0:16] * value, at_l[16:32] * value]
            left.append(jnp.concatenate(pieces, axis=0))
            right.append(at_x)
        added += dot(jnp.concatenate(left, axis=1), jnp.concatenate(right, axis=1), NT)
    place = iota((4, LANES), 0)
    place = jnp.where(place < 2, place - 2, place + CX - 2)
    gap = jnp.abs(place - iota((4, LANES), 1))
    stencil = jnp.where(gap == 1, 16.0, jnp.where(gap == 2, -1.0, 0.0))
    added += dot(near_x[...], stencil, TN, HIGHEST) * (1.0 / 12.0)
    added = added.reshape(COMP, CZ, CY, CX)
    copies = []
    for c in range(COMP):
        staged[c] = partial[c] + HALF_STEP * added[c]
        copy = pltpu.make_async_copy(staged.at[c], out.at[c], sems.at[c])
        copy.start()
        copies.append(copy)
    for copy in copies:
        copy.wait()


def call(kernel, outs, scratch=(), smem=(), count=0, whole=(), kept=()):
    def spec(k, small=(), large=()):
        space = pltpu.SMEM if k in small else pl.ANY if k in large else pltpu.VMEM
        return pl.BlockSpec(memory_space=space)

    single = not isinstance(outs, tuple)
    results = (outs,) if single else outs
    out_specs = tuple(spec(k, large=kept) for k in range(len(results)))
    return pl.pallas_call(
        kernel,
        out_shape=outs,
        in_specs=[spec(k, smem, whole) for k in range(count)],
        out_specs=out_specs[0] if single else out_specs,
        scratch_shapes=scratch,
        name=getattr(kernel, "func", kernel).__name__,
        compiler_params=pltpu.CompilerParams(vmem_limit_bytes=VMEM_GRANT),
    )


def shape(dims, dtype=F32):
    return jax.ShapeDtypeStruct(dims, dtype)


def exchanges(axis):
    count = lax.axis_size(axis)
    near = [(i, i ^ 1) for i in range(count)]
    upward = [(i, i + 1) for i in range(1, count - 1, 2)]
    return near, upward + [(b, a) for a, b in upward]


def neighbours(axis):
    count = lax.axis_size(axis)
    forward = [(i, i + 1) for i in range(count - 1)]
    return forward, [(b, a) for a, b in forward]


def shards(
    field_h,
    field_p,
    potential,
    coupling,
    wt_cells,
    wt_coords,
    wt_patch,
    patch_coef,
    sph_points,
    sph_cells,
    sph_frac,
):
    z_count = lax.axis_size("gz")
    height = lax.axis_size("gy")
    patch = wt_patch.reshape(SLOTS)
    even = lax.axis_index("gz") % 2 == 0
    core = (lax.axis_index(("gx", "gy")) + jnp.where(even, 0, PLANE)).reshape(1)
    xy_count = lax.axis_size("gx") * lax.axis_size("gy")
    near, far = neighbours("gz")
    top = field_h[:, CZ - 2 :].astype(BF16).reshape(ROWS_SLAB, LANES)
    bottom = field_h[:, :2].astype(BF16).reshape(ROWS_SLAB, LANES)
    za = lax.ppermute(top, "gz", near)
    zb = lax.ppermute(bottom, "gz", far)
    wide, plan, node, main, rest, high, low, series, target = call(
        prep_kernel,
        (
            shape((2, CX, LANES), BF16),
            shape((104, LANES)),
            shape((3, LANES)),
            shape((16, LANES), BF16),
            shape((4, LANES)),
            shape((SLOTS, CHEB * CHEB, LANES), BF16),
            shape((SLOTS, CHEB * CHEB, LANES), BF16),
            shape((3, CHEB * SLOTS, LANES)),
            shape((2, SLOTS, LANES)),
        ),
        count=11,
        smem=(0,),
    )(
        core,
        sph_cells,
        sph_frac,
        sph_points.reshape(1, LANES),
        patch_coef[0],
        jnp.moveaxis(wt_coords[0, 0, 0], 1, 0),
        wt_cells[0, 0, 0],
        field_p,
        potential,
        coupling,
        patch,
    )
    slab = shape((ROWS_SLAB, LANES), BF16)
    pad = pltpu.VMEM((ROWS_SLAB, LANES), F32)
    cube = shape((COMP, CZ, CY, CX))
    stage = [pltpu.VMEM((COMP, CZ, CY, CX), F32), pltpu.SemaphoreType.DMA((COMP,))]
    section_h, base = call(
        base_kernel, (cube, cube), scratch=stage, count=4, smem=(3,), kept=(0,)
    )(field_h, field_p, potential, coupling)
    first, last, far = call(
        functools.partial(edges_kernel, height),
        (slab, slab, shape((xy_count, 16, LANES), BF16)),
        scratch=[pad, pad],
        count=6,
        smem=(0,),
        whole=(4, 5),
    )(core, field_h, za, zb, base, plan)
    far = lax.all_to_all(far, ("gx", "gy"), 0, 0, tiled=True)
    near, distant = exchanges("gy")
    ya = lax.ppermute(first, "gy", near)
    yb = lax.ppermute(last, "gy", distant)
    inner, partial = call(
        middle_kernel, (shape((COMP, LANES)), cube), count=9, smem=(0,)
    )(core, field_h, za, zb, ya, yb, wide, plan, base)
    packed, near_x = call(
        functools.partial(pack_kernel, height),
        (shape((z_count, SENT_ROWS, LANES), BF16), shape((4, ROWS_OWN))),
        count=7,
        smem=(0,),
    )(core, inner, far, plan, node, main, rest)
    arrived = lax.all_to_all(packed, "gz", 0, 0, tiled=True)
    partner = lax.ppermute(arrived, "gy", [(i, i ^ 1) for i in range(lax.axis_size("gy"))])
    radial, angular = mode_factors()
    sent = call(
        partial_modes_kernel,
        shape((xy_count, MODE_ROWS, LANES), BF16),
        scratch=[
            pltpu.VMEM((MODE_ROWS, LANES), F32),
        ],
        count=3,
    )(arrived, jnp.asarray(radial), jnp.asarray(angular))
    gathered = lax.all_to_all(sent, ("gx", "gy"), 0, 0, tiled=True)
    section_p = call(
        source_kernel,
        cube,
        scratch=[
            pltpu.VMEM((SLOTS * 40, LANES), F32),
            pltpu.VMEM((SLOTS * COMP, LANES), F32),
            *stage,
        ],
        count=10,
        smem=(0, 1),
        kept=(0,),
    )(
        core,
        patch,
        arrived,
        partner,
        high,
        low,
        series,
        target,
        partial,
        near_x,
    )
    modes = call(sum_modes_kernel, shape((COMP, 1, NMODE)), count=1)(gathered)
    return section_h, section_p, jnp.moveaxis(modes, 1, 0)


def solution(mesh):
    placed = (
        P(None, "gz", "gy", "gx"),
        P(None, "gz", "gy", "gx"),
        P("gz", "gy", "gx"),
        P(),
        P("gz", "gy", "gx", None, None),
        P("gz", "gy", "gx", None, None, None),
        P("gz", "gy", "gx", None, None),
        P("gz", None, None, None),
        P(("gx", "gy", "gz")),
        P(None, ("gx", "gy", "gz")),
        P(None, ("gx", "gy", "gz")),
    )
    return jax.shard_map(
        shards,
        mesh=mesh,
        in_specs=placed,
        out_specs=(P(None, "gz", "gy", "gx"), P(None, "gz", "gy", "gx"), P("gz", None, None)),
        check_vma=False,
    )
```
